32 devices in a mesh: pipe: 8 (over y, x, core), expert: 4 (over z).
Axes of the slice: x: 2, y: 2, z: 4, core: 2. Of those that a mesh axis runs over, the one named last changes fastest.
Arguments:
- tokens: bfloat16 [8, 256, 3584], P('pipe', 'expert'), may hold values from -6 to 6
- cotangent: bfloat16 [8, 256, 3584], P('pipe', 'expert'), may hold values from -6 to 6
- router_gate: float32 [8, 256], P('pipe', 'expert'), may hold values from 0.3 to 1
- routes: int32 [8, 256, 1], P('pipe', 'expert'), may hold values from 0 to 1; in each aligned block of 64 rows (0 to 63, 64 to 127, ..., all dimensions but the last counted through in order) at most 34 rows name the same one
- up_weight: bfloat16 [8, 3584, 2048], P('pipe', None, 'expert'), as said below
- down_weight: bfloat16 [8, 2048, 3584], P('pipe', 'expert'), as said below
Outputs:
- input_grad: bfloat16 [8, 256, 3584], P('pipe', 'expert')
- grad_up: bfloat16 [8, 1792, 2048], P('pipe', None, 'expert')
- grad_down: bfloat16 [8, 2048, 1792], P('pipe', 'expert')
The draws below stay inside these ranges and needn't reach their ends.
Inputs may be any that keep to these rules, and one draw needn't show every extreme that they name: `routes`: among the 64 tokens of one device no expert is named more than 34 times, and some device names some expert exactly 34 times. up_weight[p] equals up_weight[7 - p]. down_weight[p] equals down_weight[7 - p].
All inputs are finite; a program needn't handle non-finite values.
Results may differ from the reference program's by a relative error of at most 0.0085.
Values may be sent and summed in bfloat16 or wider, within the bound.
No kernel may reach another device: no remote copies, remote signals or barrier semaphores. Data moves between devices by JAX's collectives and lax.ppermute only.
A program may use at most 64 MiB of HBM per device.

```python
import math
import jax
import jax.numpy as jnp
import numpy as np
from jax import lax

D = 3584
EXP_HIDDEN = 1024
EXPERTS = 2
TOK_DEV = 64
CAP = 34
RANKS = 8
SECTIONS = 4
N_PIPE = 8
N_EXPERT = 4


def mirrored(key, shape, fan_in):
    base = jax.random.normal(key, shape, jnp.float32)
    base = base * fan_in ** (-0.5)
    return jnp.concatenate([base, base[::-1]], axis=0)


def draw_up_weight(key, part):
    return mirrored(jax.random.fold_in(key, 11), (SECTIONS, D, EXPERTS * EXP_HIDDEN), D).astype(jnp.bfloat16)


def draw_down_weight(key, part):
    return mirrored(jax.random.fold_in(key, 23), (SECTIONS, EXPERTS * EXP_HIDDEN, D), EXP_HIDDEN).astype(jnp.bfloat16)


def steps_of(rng, shape, pieces, smallest, top_value):
    factor_of = 1.0
    for dim, shards_of in pieces:
        steps = jax.random.uniform(jax.random.fold_in(jax.random.fold_in(rng, 6), dim), (shards_of,), jnp.float32, smallest / len(pieces), top_value / len(pieces))
        factor_of = factor_of * jnp.repeat(jnp.exp(steps), shape[dim] // shards_of).reshape((-1,) + (1,) * (len(shape) - 1 - dim))
    return factor_of


def deal_out(key, own, number, rows, count, top, bound, skew):
    sequence = jax.random.permutation(key, count)
    crowded, common = portions_of(count, rows * top, bound, skew, True), portions_of(count, rows * top, bound, skew, False)
    places = jnp.arange(count)

    def named(lengths, offset_by):
        used = int((lengths > 0).sum())
        fixed = max(1, used // 4)
        shifted = fixed + (places - fixed + offset_by * (used - fixed)) % max(1, count - fixed)
        return jnp.zeros((count,), jnp.int32).at[sequence[jnp.where(places < fixed, places, shifted)]].set(jnp.asarray(lengths, jnp.int32))

    lengths = jnp.where(number % 4 == 0, named(crowded, number // 4), named(common, number - number // 4 - 1))
    mixed = jax.random.permutation(jax.random.fold_in(own, 3), count)
    donor, sink = mixed[0:count // 2 * 2:2], mixed[1:count // 2 * 2:2]
    slack = jnp.minimum(lengths[donor] - 1, bound - lengths[sink]) // 2
    slack = jnp.where((donor == sequence[0]) | (sink == sequence[0]) | (lengths[sink] == 0), 0, jnp.maximum(slack, 0))
    shifted = jax.random.randint(jax.random.fold_in(own, 4), (count // 2,), 0, 1 << 20) % (slack + 1)
    lengths = lengths.at[donor].add(-shifted).at[sink].add(shifted)
    members = jnp.searchsorted(jnp.cumsum(lengths), jnp.arange(rows * top), side="right").astype(jnp.int32)
    listing = members.reshape(top, rows).T
    listing = listing[jax.random.permutation(jax.random.fold_in(own, 1), rows)]
    offset_by = jax.random.randint(jax.random.fold_in(own, 2), (rows, 1), 0, top)
    return jnp.take_along_axis(listing, (jnp.arange(top)[None, :] + offset_by) % top, axis=1)


def portions_of(amount, total, reach, lean, full):
    weights = [(1 << 20) // math.isqrt(standing ** lean) + 1 for standing in range(1, amount + 1)]
    largest = reach if full else min(reach, max(-(-total // amount), total * weights[0] // sum(weights)))
    least = 1 if total - largest >= amount - 1 else 0
    holding, rest = [largest] + [least] * (amount - 1), total - largest - least * (amount - 1)
    while rest > 0:
        candidates = [i for i in range(1, amount) if holding[i] < largest] or [i for i in range(1, amount) if holding[i] < reach]
        mass, remaining = sum([weights[i] for i in candidates]), rest
        for i in candidates:
            more = min(reach - holding[i], max(1, remaining * weights[i] // mass), rest)
            holding[i] = holding[i] + more
            rest = rest - more
    return np.array(holding)


def normal_values(own_key, extent, deviation, most, cuts=(), held_as=jnp.bfloat16):
    entries = jax.random.normal(own_key, extent, jnp.float32) * deviation
    if len(cuts) > 0:
        entries = steps_of(own_key, extent, cuts, -0.22, 0.18) * entries
    return jnp.clip(entries, min=-most, max=most).astype(held_as)


def setup_inputs(seed: int = 0) -> dict:
    key_of = jax.random.split(jax.random.key(seed), 7)
    tokens = normal_values(key_of[0], (RANKS, N_EXPERT * TOK_DEV, D), 1.0, 6.0, ((0, 8), (1, 4)))
    cotangent = normal_values(key_of[1], (RANKS, N_EXPERT * TOK_DEV, D), 1.0, 6.0, ((0, 8), (1, 4)))
    router_gate = jnp.clip(jnp.exp(math.log(1.0) - 1.2039728 * jax.random.uniform(key_of[2], (RANKS, N_EXPERT * TOK_DEV), jnp.float32) ** steps_of(key_of[2], (RANKS, N_EXPERT * TOK_DEV), ((0, 8), (1, 4)), -0.2, 0.2)), 0.3, 1.0)
    routes_keys = jax.random.split(jax.random.fold_in(key_of[3], 1), RANKS * (N_EXPERT * TOK_DEV) // TOK_DEV)
    routes_turns = jax.random.permutation(jax.random.fold_in(key_of[3], 3), RANKS * (N_EXPERT * TOK_DEV) // TOK_DEV)
    routes = jax.vmap(lambda own, number: deal_out(jax.random.fold_in(key_of[3], 2), own, number, TOK_DEV, EXPERTS, 1, CAP, 2))(routes_keys, routes_turns).reshape((RANKS, N_EXPERT * TOK_DEV, 1))
    up_weight = draw_up_weight(jax.random.fold_in(key_of[6], 71), 0)
    down_weight = draw_down_weight(jax.random.fold_in(key_of[6], 71), 0)
    return {"tokens": tokens, "cotangent": cotangent, "router_gate": router_gate, "routes": routes, "up_weight": up_weight, "down_weight": down_weight}


def slot_numbers(route_ids):
    member = (route_ids[..., None] == jnp.arange(EXPERTS, dtype=jnp.int32)).astype(jnp.int32)
    before = jnp.cumsum(member, axis=-2) - member
    return jnp.sum(before * member, axis=-1)


def placement(route_ids):
    slots = slot_numbers(route_ids)
    expert_hit = route_ids[:, None, None, :] == jnp.arange(EXPERTS, dtype=jnp.int32)[None, :, None, None]
    slot_hit = slots[:, None, None, :] == jnp.arange(CAP, dtype=jnp.int32)[None, None, :, None]
    return jnp.logical_and(expert_hit, slot_hit).astype(jnp.float32)


def rank_work(rank_tokens, rank_cot, rank_gate, rank_routes, rank_up, rank_down):
    owners = N_EXPERT
    group = N_EXPERT // EXPERTS
    slice_width = EXP_HIDDEN // group
    row_count = owners * CAP
    local_x = rank_tokens.reshape(owners, TOK_DEV, D)
    scaled = (rank_gate.reshape(owners, TOK_DEV, 1) * rank_cot.reshape(owners, TOK_DEV, D).astype(jnp.float32)).astype(jnp.bfloat16)
    places = placement(rank_routes.reshape(owners, TOK_DEV))
    routed_x = jnp.einsum("qect,qtd->eqcd", places, local_x.astype(jnp.float32)).astype(jnp.bfloat16)
    routed_g = jnp.einsum("qect,qtd->eqcd", places, scaled.astype(jnp.float32)).astype(jnp.bfloat16)
    up_terms = []
    down_terms = []
    combined = []
    for expert_id in range(EXPERTS):
        rows_x = routed_x[expert_id].reshape(row_count, D)
        rows_g = routed_g[expert_id].reshape(row_count, D)
        up_cols = rank_up[:, expert_id * EXP_HIDDEN:(expert_id + 1) * EXP_HIDDEN]
        down_rows = rank_down[expert_id * EXP_HIDDEN:(expert_id + 1) * EXP_HIDDEN, :]
        pre = jnp.dot(rows_x, up_cols, preferred_element_type=jnp.float32)
        act = jax.nn.silu(pre).astype(jnp.bfloat16)
        dact = jnp.dot(rows_g, down_rows.T, preferred_element_type=jnp.float32)
        sigma = jax.nn.sigmoid(pre)
        dpre = (dact * sigma * (1.0 + pre * (1.0 - sigma))).astype(jnp.bfloat16)
        up_terms.append(jnp.dot(rows_x.T, dpre, preferred_element_type=jnp.float32).astype(jnp.bfloat16))
        down_terms.append(jnp.dot(act.T, rows_g, preferred_element_type=jnp.float32).astype(jnp.bfloat16))
        part_dx = jnp.einsum("rgh,dgh->grd", dpre.reshape(row_count, group, slice_width).astype(jnp.float32), up_cols.reshape(D, group, slice_width).astype(jnp.float32)).astype(jnp.bfloat16)
        summed = jnp.sum(part_dx.astype(jnp.float32), axis=0)
        combined.append(summed.reshape(owners, CAP, D))
    stacked = jnp.stack(combined, axis=1)
    input_grad = jnp.einsum("qect,qecd->qtd", places, stacked, precision=lax.Precision.HIGHEST).astype(jnp.bfloat16)
    return input_grad.reshape(owners * TOK_DEV, D), jnp.concatenate(up_terms, axis=1), jnp.concatenate(down_terms, axis=0)


def reference(tokens, cotangent, router_gate, routes, up_weight, down_weight):
    def one_rank(rank_id):
        return rank_work(tokens[rank_id], cotangent[rank_id], router_gate[rank_id], routes[rank_id, :, 0], up_weight[rank_id], down_weight[rank_id])

    input_grad, rank_up, rank_down = lax.map(one_rank, jnp.arange(N_PIPE, dtype=jnp.int32))
    total_up = (rank_up.astype(jnp.float32) + rank_up[::-1].astype(jnp.float32)).astype(jnp.bfloat16)
    total_down = (rank_down.astype(jnp.float32) + rank_down[::-1].astype(jnp.float32)).astype(jnp.bfloat16)
    sections = N_PIPE // 2
    half = D // 2
    grad_up = jnp.concatenate([total_up[:sections, :half], total_up[sections:, half:]], axis=0)
    grad_down = jnp.concatenate([total_down[:sections, :, :half], total_down[sections:, :, half:]], axis=0)
    return input_grad, grad_up, grad_down
```

```python
import functools

import jax
import jax.numpy as jnp
from jax import lax
from jax.experimental import pallas as pl
from jax.experimental.pallas import tpu as pltpu
from jax.sharding import PartitionSpec as P

EXPERTS = 2
CAP = 34
FOLD = 8
MAIN = CAP // FOLD * FOLD
REM = CAP - MAIN
CHUNKS = FOLD // REM
VMEM_LIMIT = 24 * 1024 * 1024
F32 = jnp.float32
BF16 = jnp.bfloat16


def dot(a, b, dims=((1,), (0,))):
    return lax.dot_general(a, b, (dims, ((), ())), preferred_element_type=F32)


def vmem():
    return pl.BlockSpec(memory_space=pltpu.VMEM)


def smem():
    return pl.BlockSpec(memory_space=pltpu.SMEM)


def call(kernel, outs, flops, moved, name, **more):
    return functools.partial(
        pl.pallas_call,
        kernel,
        out_shape=outs,
        name=name,
        compiler_params=pltpu.CompilerParams(vmem_limit_bytes=VMEM_LIMIT),
        cost_estimate=pl.CostEstimate(flops=flops, bytes_accessed=moved, transcendentals=0),
        **more,
    )()


def route_masks(mine_ref, routes_ref):
    routes = routes_ref[...]
    tok = routes.shape[1]
    own = routes == mine_ref[0]
    own_f = jnp.where(own, 1.0, 0.0).astype(F32)
    earlier = lax.broadcasted_iota(jnp.int32, (tok, tok), 0) < lax.broadcasted_iota(jnp.int32, (tok, tok), 1)
    count_own = dot(jnp.broadcast_to(own_f, (8, tok)).astype(BF16), jnp.where(earlier, 1.0, 0.0).astype(BF16))[0:1]
    index = lax.broadcasted_iota(jnp.int32, (1, tok), 1)
    count_own = count_own.astype(jnp.int32)
    slot = jnp.where(own, count_own, index - count_own)
    rows = 2 * MAIN + 2 * FOLD
    row = lax.broadcasted_iota(jnp.int32, (rows, tok), 0)
    slot = jnp.broadcast_to(slot, (rows, tok))
    own = jnp.broadcast_to(jnp.where(own, 1, 0), (rows, tok))
    side = jnp.where(row < 2 * MAIN, row // MAIN, (row - 2 * MAIN) // FOLD)
    place = lax.rem(row, FOLD)
    hit_side = own == 1 - side
    masks = []
    for chunk in range(CHUNKS):
        folded = jnp.where(place // REM == chunk, MAIN + lax.rem(place, REM), -1)
        wanted = jnp.where(row < 2 * MAIN, lax.rem(row, MAIN), folded)
        masks.append(jnp.where(jnp.logical_and(hit_side, slot == wanted), 1.0, 0.0).astype(BF16))
    return masks


def split_rows(masks, source, own_ref, other_ref):
    width = source.shape[1] // CHUNKS
    fold_own = fold_other = None
    for chunk in range(CHUNKS):
        part = dot(masks[chunk], source[:, chunk * width:(chunk + 1) * width])
        own_ref[chunk * MAIN:(chunk + 1) * MAIN, :] = part[:MAIN].astype(BF16)
        other_ref[chunk * MAIN:(chunk + 1) * MAIN, :] = part[MAIN:2 * MAIN].astype(BF16)
        a, b = part[2 * MAIN:2 * MAIN + FOLD], part[2 * MAIN + FOLD:]
        fold_own = a if fold_own is None else fold_own + a
        fold_other = b if fold_other is None else fold_other + b
    own_ref[CHUNKS * MAIN:, :] = fold_own.astype(BF16)
    other_ref[CHUNKS * MAIN:, :] = fold_other.astype(BF16)


def route_x_kernel(mine_ref, routes_ref, tokens_ref, own_ref, other_ref):
    split_rows(route_masks(mine_ref, routes_ref), tokens_ref[...], own_ref, other_ref)


def route_g_kernel(mine_ref, routes_ref, gate_ref, cot_ref, own_ref, other_ref):
    tok = gate_ref.shape[1]
    eye = lax.broadcasted_iota(jnp.int32, (tok, tok), 0) == lax.broadcasted_iota(jnp.int32, (tok, tok), 1)
    gate = jnp.sum(jnp.where(eye, jnp.broadcast_to(gate_ref[...], (tok, tok)), 0.0), axis=1, keepdims=True)
    scaled = (gate * cot_ref[...].astype(F32)).astype(BF16)
    split_rows(route_masks(mine_ref, routes_ref), scaled, own_ref, other_ref)


def fold_pick(owners, chunk):
    shape = (owners * REM, owners * FOLD)
    row = lax.broadcasted_iota(jnp.int32, shape, 0)
    col = lax.broadcasted_iota(jnp.int32, shape, 1)
    want = row // REM * FOLD + chunk * REM + lax.rem(row, REM)
    return jnp.where(col == want, 1.0, 0.0).astype(BF16)


def join_rows(payloads, rows_ref):
    owners = len(payloads)
    folds = jnp.concatenate([ref[CHUNKS * MAIN:, :].astype(F32) for ref in payloads], axis=0).astype(BF16)
    for chunk in range(CHUNKS):
        for r, ref in enumerate(payloads):
            rows_ref[chunk, r * MAIN:(r + 1) * MAIN, :] = ref[chunk * MAIN:(chunk + 1) * MAIN, :]
        rows_ref[chunk, owners * MAIN:, :] = dot(fold_pick(owners, chunk), folds).astype(BF16)


def pre_kernel(owners, upper_ref, *refs):
    payloads, (up_ref, pre_ref, keep_ref, send_ref, rows) = refs[:owners], refs[owners:]
    join_rows(payloads, rows)
    half = CHUNKS // 2
    upper = upper_ref[0]
    keep_ref[...] = rows[pl.ds(upper * half, half)]
    send_ref[...] = rows[pl.ds((1 - upper) * half, half)]
    width = rows.shape[2]
    total = None
    for chunk in range(CHUNKS):
        part = dot(rows[chunk], up_ref[chunk * width:(chunk + 1) * width, :])
        total = part if total is None else total + part
    pre_ref[...] = total


def join_g_kernel(owners, upper_ref, *refs):
    payloads, (rows_ref, keep_ref, send_ref) = refs[:owners], refs[owners:]
    join_rows(payloads, rows_ref)
    half = CHUNKS // 2
    upper = upper_ref[0]
    keep_ref[...] = rows_ref[pl.ds(upper * half, half)]
    send_ref[...] = rows_ref[pl.ds((1 - upper) * half, half)]


def hidden_kernel(rows_ref, pre_ref, down_ref, hidden_ref):
    width = rows_ref.shape[2]
    total = None
    for chunk in range(CHUNKS):
        part = dot(rows_ref[chunk], down_ref[:, chunk * width:(chunk + 1) * width], ((1,), (1,)))
        total = part if total is None else total + part
    pre = pre_ref[...]
    sigma = 1.0 / (1.0 + jnp.exp(-pre))
    hidden_ref[0] = (total * sigma * (1.0 + pre * (1.0 - sigma))).astype(BF16)
    hidden_ref[1] = (pre * sigma).astype(BF16)


def back_kernel(owners, hidden_ref, up_ref, *outs):
    dpre = hidden_ref[0]
    width = up_ref.shape[0] // CHUNKS
    folds = None
    for chunk in range(CHUNKS):
        part = dot(dpre, up_ref[chunk * width:(chunk + 1) * width, :], ((1,), (1,))).astype(BF16)
        for r in range(owners):
            outs[r][chunk * MAIN:(chunk + 1) * MAIN, :] = part[r * MAIN:(r + 1) * MAIN]
        fold = dot(fold_pick(owners, chunk), part[owners * MAIN:], ((0,), (0,)))
        folds = fold if folds is None else folds + fold
    for r in range(owners):
        outs[r][CHUNKS * MAIN:, :] = folds[r * FOLD:(r + 1) * FOLD].astype(BF16)


def grad_kernel(hid_a, hid_b, xa, xb, ga, gb, up_ref, down_ref):
    step = pl.program_id(0)
    del step
    t = ((0,), (0,))
    up_ref[...] = (dot(xa[0], hid_a[0], t) + dot(xb[0], hid_b[0], t)).astype(BF16)
    down_ref[...] = (dot(hid_a[1], ga[0], t) + dot(hid_b[1], gb[0], t)).astype(BF16)


def final_kernel(owners, group, mine_ref, routes_ref, *refs):
    parts, out_ref = refs[:owners], refs[owners]
    masks = route_masks(mine_ref, routes_ref)
    width = out_ref.shape[1] // CHUNKS

    def sides(lo, hi):
        own = sum(ref[lo:hi, :].astype(F32) for ref in parts[:group])
        other = sum(ref[lo:hi, :].astype(F32) for ref in parts[group:])
        return [own, other]

    folds = sides(CHUNKS * MAIN, CHUNKS * MAIN + FOLD)
    for chunk in range(CHUNKS):
        rows = jnp.concatenate(sides(chunk * MAIN, (chunk + 1) * MAIN) + folds, axis=0).astype(BF16)
        out_ref[:, chunk * width:(chunk + 1) * width] = dot(masks[chunk], rows, ((0,), (0,))).astype(BF16)


def per_device(tokens, cotangent, router_gate, routes, up_weight, down_weight):
    owners = lax.axis_size("expert")
    ranks = lax.axis_size("pipe")
    group = owners // EXPERTS
    tok, model = tokens.shape[1:]
    hidden = up_weight.shape[2]
    width = model // CHUNKS
    rows = owners * CAP
    half = CHUNKS // 2
    mine = (lax.axis_index("expert") // group).astype(jnp.int32).reshape(1)
    upper = (lax.axis_index("pipe") >= ranks // 2).astype(jnp.int32).reshape(1)
    ids = routes.reshape(1, tok)
    up, down = up_weight[0], down_weight[0]

    payload = jax.ShapeDtypeStruct((CHUNKS * MAIN + FOLD, width), BF16)
    halves = jax.ShapeDtypeStruct((half, rows, width), BF16)

    def swap(value, r):
        return lax.ppermute(value, "expert", [(q, q ^ r) for q in range(owners)])

    def mirror(value):
        return lax.ppermute(value, "pipe", [(i, ranks - 1 - i) for i in range(ranks)])

    def deal(own, other):
        got = {r: swap(own if r < group else other, r) for r in reversed(range(1, owners))}
        return [own] + [got[r] for r in range(1, owners)]

    small = 1 << 20
    x_own, x_other = call(
        route_x_kernel, (payload, payload), small, small, "route_x", in_specs=[smem(), vmem(), vmem()], out_specs=(vmem(), vmem())
    )(mine, ids, tokens[0])
    x_parts = deal(x_own, x_other)
    g_own, g_other = call(
        route_g_kernel, (payload, payload), small, small, "route_g", in_specs=[smem()] + [vmem()] * 3, out_specs=(vmem(), vmem())
    )(mine, ids, router_gate, cotangent[0])
    g_parts = deal(g_own, g_other)

    flops = 2 * rows * model * hidden
    moved = 2 * model * hidden
    pre, x_keep, x_send = call(
        functools.partial(pre_kernel, owners),
        (jax.ShapeDtypeStruct((rows, hidden), F32), halves, halves),
        flops, moved, "pre",
        in_specs=[smem()] + [vmem()] * (owners + 1),
        out_specs=(vmem(),) * 3,
        scratch_shapes=[pltpu.VMEM((CHUNKS, rows, width), BF16)],
    )(upper, *x_parts, up)
    x_far = mirror(x_send)
    g_rows, g_keep, g_send = call(
        functools.partial(join_g_kernel, owners),
        (jax.ShapeDtypeStruct((CHUNKS, rows, width), BF16), halves, halves),
        small, small, "join_g",
        in_specs=[smem()] + [vmem()] * owners,
        out_specs=(vmem(),) * 3,
    )(upper, *g_parts)
    g_far = mirror(g_send)
    hid = call(
        hidden_kernel, jax.ShapeDtypeStruct((2, rows, hidden), BF16), flops, moved, "hidden", in_specs=[vmem()] * 3, out_specs=vmem()
    )(g_rows, pre, down)
    hid_far = mirror(hid)
    back = call(
        functools.partial(back_kernel, owners), (payload,) * owners, flops, moved, "back",
        in_specs=[vmem()] * 2, out_specs=(vmem(),) * owners,
    )(hid, up)
    got = {r: swap(back[r], r) for r in reversed(range(1, owners))}
    back_parts = [back[0]] + [got[r] for r in range(1, owners)]

    whole = pl.BlockSpec((2, rows, hidden), lambda k: (0, 0, 0))
    chunk = pl.BlockSpec((1, rows, width), lambda k: (k, 0, 0))
    grad_up, grad_down = call(
        grad_kernel,
        (jax.ShapeDtypeStruct((model // 2, hidden), BF16), jax.ShapeDtypeStruct((hidden, model // 2), BF16)),
        2 * flops, moved, "grad",
        grid=(half,),
        in_specs=[whole, whole] + [chunk] * 4,
        out_specs=(pl.BlockSpec((width, hidden), lambda k: (k, 0)), pl.BlockSpec((hidden, width), lambda k: (0, k))),
    )(hid, hid_far, x_keep, x_far, g_keep, g_far)
    input_grad = call(
        functools.partial(final_kernel, owners, group), jax.ShapeDtypeStruct((tok, model), BF16), small, small, "final",
        in_specs=[smem()] + [vmem()] * (owners + 1), out_specs=vmem(),
    )(mine, ids, *back_parts)
    return (input_grad[None], grad_up[None], grad_down[None])


def solution(mesh):
    placed = (
        P("pipe", "expert", None),
        P("pipe", "expert", None),
        P("pipe", "expert"),
        P("pipe", "expert", None),
        P("pipe", None, "expert"),
        P("pipe", "expert", None),
    )
    return jax.shard_map(
        per_device,
        mesh=mesh,
        in_specs=placed,
        out_specs=(P("pipe", "expert", None), P("pipe", None, "expert"), P("pipe", "expert", None)),
        check_vma=False,
    )
```

```python
import functools

import jax
import jax.numpy as jnp
from jax import lax
from jax.experimental import pallas as pl
from jax.experimental.pallas import tpu as pltpu
from jax.sharding import PartitionSpec as P


EXPERTS = 2
CAP = 34
FOLD = 8
MAIN = CAP // FOLD * FOLD
REM = CAP - MAIN
CHUNKS = FOLD // REM
LINE = 4
VMEM_LIMIT = 24 * 1024 * 1024
F32 = jnp.float32
BF16 = jnp.bfloat16


def dot(a, b, dims=((1,), (0,))):
    return lax.dot_general(a, b, (dims, ((), ())), preferred_element_type=F32)


def vmem():
    return pl.BlockSpec(memory_space=pltpu.VMEM)


def smem():
    return pl.BlockSpec(memory_space=pltpu.SMEM)


def in_hbm(value):
    return pltpu.with_memory_space_constraint(value, pltpu.HBM)


def call(kernel, outs, flops, moved, **more):
    return pl.pallas_call(
        kernel,
        out_shape=outs,
        compiler_params=pltpu.CompilerParams(vmem_limit_bytes=VMEM_LIMIT),
        cost_estimate=pl.CostEstimate(flops=flops, bytes_accessed=moved, transcendentals=0),
        **more,
    )


def route_masks(mine_ref, routes_ref):
    routes = routes_ref[...]
    tok = routes.shape[1]
    own = routes == mine_ref[0]
    own_f = jnp.where(own, 1.0, 0.0).astype(F32)
    earlier = lax.broadcasted_iota(jnp.int32, (tok, tok), 0) < lax.broadcasted_iota(jnp.int32, (tok, tok), 1)
    count_own = dot(jnp.broadcast_to(own_f, (8, tok)).astype(BF16), jnp.where(earlier, 1.0, 0.0).astype(BF16))[0:1]
    index = lax.broadcasted_iota(jnp.int32, (1, tok), 1)
    count_own = count_own.astype(jnp.int32)
    slot = jnp.where(own, count_own, index - count_own)
    rows = 2 * MAIN + 2 * FOLD
    row = lax.broadcasted_iota(jnp.int32, (rows, tok), 0)
    slot = jnp.broadcast_to(slot, (rows, tok))
    own = jnp.broadcast_to(jnp.where(own, 1, 0), (rows, tok))
    side = jnp.where(row < 2 * MAIN, row // MAIN, (row - 2 * MAIN) // FOLD)
    place = lax.rem(row, FOLD)
    hit_side = own == 1 - side
    masks = []
    for chunk in range(CHUNKS):
        folded = jnp.where(place // REM == chunk, MAIN + lax.rem(place, REM), -1)
        wanted = jnp.where(row < 2 * MAIN, lax.rem(row, MAIN), folded)
        masks.append(jnp.where(jnp.logical_and(hit_side, slot == wanted), 1.0, 0.0).astype(BF16))
    return masks


def split_rows(masks, source, own_ref, other_ref):
    width = source.shape[1] // CHUNKS
    fold_own = fold_other = None
    for chunk in range(CHUNKS):
        part = dot(masks[chunk], source[:, chunk * width:(chunk + 1) * width])
        own_ref[chunk * MAIN:(chunk + 1) * MAIN, :] = part[:MAIN].astype(BF16)
        other_ref[chunk * MAIN:(chunk + 1) * MAIN, :] = part[MAIN:2 * MAIN].astype(BF16)
        a, b = part[2 * MAIN:2 * MAIN + FOLD], part[2 * MAIN + FOLD:]
        fold_own = a if fold_own is None else fold_own + a
        fold_other = b if fold_other is None else fold_other + b
    own_ref[CHUNKS * MAIN:, :] = fold_own.astype(BF16)
    other_ref[CHUNKS * MAIN:, :] = fold_other.astype(BF16)


def hbm():
    return pl.BlockSpec(memory_space=pltpu.HBM)


def route_kernel(mine_ref, ids_hbm, gate_hbm, tokens_hbm, cot_hbm, x_own, x_other, g_own, g_other, ids, gate, tokens, cot, sems):
    copies = [
        pltpu.make_async_copy(src, dst, sems.at[i])
        for i, (src, dst) in enumerate([(ids_hbm, ids), (tokens_hbm, tokens), (gate_hbm, gate), (cot_hbm, cot)])
    ]
    for copy in copies:
        copy.start()
    copies[0].wait()
    masks = route_masks(mine_ref, ids)
    copies[1].wait()
    split_rows(masks, tokens[...], x_own, x_other)
    tok = gate.shape[1]
    eye = lax.broadcasted_iota(jnp.int32, (tok, tok), 0) == lax.broadcasted_iota(jnp.int32, (tok, tok), 1)
    copies[2].wait()
    column = jnp.sum(jnp.where(eye, jnp.broadcast_to(gate[...], (tok, tok)), 0.0), axis=1, keepdims=True)
    copies[3].wait()
    scaled = (column * cot[...].astype(F32)).astype(BF16)
    split_rows(masks, scaled, g_own, g_other)


def fold_rows(count):
    return -(-count * REM // FOLD) * FOLD


def row_count(count):
    return count * MAIN + fold_rows(count)


def fold_pick(count, chunk):
    shape = (fold_rows(count), count * FOLD)
    row = lax.broadcasted_iota(jnp.int32, shape, 0)
    col = lax.broadcasted_iota(jnp.int32, shape, 1)
    want = row // REM * FOLD + chunk * REM + lax.rem(row, REM)
    return jnp.where(col == want, 1.0, 0.0).astype(BF16)


def join_rows(payloads, rows_ref, base=0):
    count = len(payloads)
    folds = jnp.concatenate([ref[CHUNKS * MAIN:, :].astype(F32) for ref in payloads], axis=0).astype(BF16)
    last = base + count * MAIN
    for chunk in range(CHUNKS):
        for r, ref in enumerate(payloads):
            rows_ref[chunk, base + r * MAIN:base + (r + 1) * MAIN, :] = ref[chunk * MAIN:(chunk + 1) * MAIN, :]
        rows_ref[chunk, last:last + fold_rows(count), :] = dot(fold_pick(count, chunk), folds).astype(BF16)


def pre_kernel(sizes, upper_ref, *refs):
    count = sum(sizes)
    payloads, (up_hbm, down_hbm, pre_ref, keep_ref, send_ref, up_ref, down_ref, rows, sems) = refs[:count], refs[count:]
    load_up = pltpu.make_async_copy(up_hbm, up_ref, sems.at[0])
    load_down = pltpu.make_async_copy(down_hbm, down_ref, sems.at[1])
    load_up.start()
    load_down.start()
    base = first = 0
    for size in sizes:
        join_rows(payloads[first:first + size], rows, base)
        first, base = first + size, base + row_count(size)
    half = CHUNKS // 2
    upper = upper_ref[0]
    keep_ref[...] = rows[pl.ds(upper * half, half)]
    send_ref[...] = rows[pl.ds((1 - upper) * half, half)]
    width = rows.shape[2]
    load_up.wait()
    total = None
    for chunk in range(CHUNKS):
        part = dot(rows[chunk], up_ref[chunk * width:(chunk + 1) * width, :])
        total = part if total is None else total + part
    pre_ref[...] = total
    load_down.wait()


def group_kernel(size, base, upper_ref, *refs):
    payloads, (pre_ref, up_ref, down_ref, keep_ref, send_ref) = refs[:size], refs[size:size + 5]
    outs, rows = refs[size + 5:-1], refs[-1]
    join_rows(payloads, rows)
    width = rows.shape[2]
    half = CHUNKS // 2
    upper = upper_ref[0]
    keep_ref[:, :, :width] = rows[pl.ds(upper * half, half)]
    send_ref[:, :, :width] = rows[pl.ds((1 - upper) * half, half)]
    dact = None
    for chunk in range(CHUNKS):
        part = dot(rows[chunk], down_ref[:, chunk * width:(chunk + 1) * width], ((1,), (1,)))
        dact = part if dact is None else dact + part
    pre = pre_ref[base:base + rows.shape[1], :]
    sigma = 1.0 / (1.0 + jnp.exp(-pre))
    dpre = (dact * sigma * (1.0 + pre * (1.0 - sigma))).astype(BF16)
    act = (pre * sigma).astype(BF16)
    for ref in (keep_ref, send_ref):
        ref[0, :, width:] = dpre
        ref[1, :, width:] = act
    folds = None
    for chunk in range(CHUNKS):
        part = dot(dpre, up_ref[chunk * width:(chunk + 1) * width, :], ((1,), (1,))).astype(BF16)
        for r in range(size):
            outs[r][chunk * MAIN:(chunk + 1) * MAIN, :] = part[r * MAIN:(r + 1) * MAIN]
        fold = dot(fold_pick(size, chunk), part[size * MAIN:], ((0,), (0,)))
        folds = fold if folds is None else folds + fold
    for r in range(size):
        outs[r][CHUNKS * MAIN:, :] = folds[r * FOLD:(r + 1) * FOLD].astype(BF16)


def add_kernel(a_ref, b_ref, out_ref):
    out_ref[...] = (a_ref[...].astype(F32) + b_ref[...].astype(F32)).astype(BF16)


def grad_kernel(groups, x_keep, x_far, *refs):
    packs, (up_ref, down_ref) = refs[:2 * groups], refs[2 * groups:]
    width = x_keep.shape[2]
    chunk = pl.program_id(0)
    across = ((0,), (0,))

    def side(x_ref, refs):
        dpre = jnp.concatenate([ref[0, :, width:] for ref in refs], axis=0)
        act = jnp.concatenate([ref[1, :, width:] for ref in refs], axis=0)
        g = jnp.concatenate([ref[chunk, :, :width] for ref in refs], axis=0)
        return dot(x_ref[0], dpre, across), dot(act, g, across)

    up_own, down_own = side(x_keep, packs[:groups])
    up_far, down_far = side(x_far, packs[groups:])
    up_ref[...] = (up_own + up_far).astype(BF16)
    down_ref[...] = (down_own + down_far).astype(BF16)


def final_kernel(own_count, mine_ref, routes_ref, *refs):
    own_refs, other_refs, out_ref = refs[:own_count], refs[own_count:-1], refs[-1]
    masks = route_masks(mine_ref, routes_ref)
    width = out_ref.shape[1] // CHUNKS

    def sides(lo, hi):
        return [sum(ref[lo:hi, :].astype(F32) for ref in side) for side in (own_refs, other_refs)]

    folds = sides(CHUNKS * MAIN, CHUNKS * MAIN + FOLD)
    for chunk in range(CHUNKS):
        rows = jnp.concatenate(sides(chunk * MAIN, (chunk + 1) * MAIN) + folds, axis=0).astype(BF16)
        out_ref[:, chunk * width:(chunk + 1) * width] = dot(masks[chunk], rows, ((0,), (0,))).astype(BF16)


def per_device(tokens, cotangent, router_gate, routes, up_weight, down_weight):
    owners = lax.axis_size("expert")
    ranks = lax.axis_size("pipe")
    group = owners // EXPERTS
    tok, model = tokens.shape[1:]
    hidden = up_weight.shape[2]
    width = model // CHUNKS
    half = CHUNKS // 2
    here = lax.axis_index("expert")
    mine = (here // group).astype(jnp.int32).reshape(1)
    upper = (lax.axis_index("pipe") >= ranks // 2).astype(jnp.int32).reshape(1)
    ids = routes.reshape(1, tok)
    up, down = up_weight[0], down_weight[0]

    line = owners == LINE
    groups = [[0, 1, 3], [2]] if line else [list(range(owners))]
    sizes = [len(sources) for sources in groups]
    rows = sum(map(row_count, sizes))

    def held(shape, dtype=BF16):
        return pltpu.VMEM(shape, dtype)

    payload = held((CHUNKS * MAIN + FOLD, width))
    halves = held((half, rows, width))

    def send(value, pairs):
        return lax.ppermute(value, "expert", pairs)

    def swap(value, r):
        return send(value, [(q, q ^ r) for q in range(owners)])

    def mirror(value):
        return lax.ppermute(value, "pipe", [(i, ranks - 1 - i) for i in range(ranks)])

    def deal(own, other):
        if not line:
            return {0: own} | {r: swap(own if r < group else other, r) for r in reversed(range(1, owners))}
        across = swap(other, 3)
        beside = swap(own, 1)
        inner = jnp.logical_and(here > 0, here < owners - 1)
        relayed = send(jnp.where(inner, across, other), [(0, 2), (3, 1), (1, 0), (2, 3)])
        return {0: own, 1: beside, 2: relayed, 3: across}

    small = 1 << 20
    x_own, x_other, g_own, g_other = call(
        route_kernel, (payload,) * 4, small, small,
        in_specs=[smem()] + [hbm()] * 4,
        out_specs=(vmem(),) * 4,
        scratch_shapes=[
            pltpu.VMEM((1, tok), jnp.int32),
            pltpu.VMEM((1, tok), F32),
            pltpu.VMEM((tok, model), BF16),
            pltpu.VMEM((tok, model), BF16),
            pltpu.SemaphoreType.DMA((4,)),
        ],
    )(mine, *map(in_hbm, (ids, router_gate, tokens[0], cotangent[0])))
    x_parts = deal(x_own, x_other)
    g_parts = deal(g_own, g_other)

    flops = 2 * rows * model * hidden
    moved = 2 * model * hidden
    pre, x_keep, x_send, up_here, down_here = call(
        functools.partial(pre_kernel, sizes),
        (held((rows, hidden), F32), halves, halves, held((model, hidden)), held((hidden, model))),
        flops, moved,
        in_specs=[smem()] + [vmem()] * owners + [hbm()] * 2,
        out_specs=(vmem(),) * 5,
        scratch_shapes=[pltpu.VMEM((CHUNKS, rows, width), BF16), pltpu.SemaphoreType.DMA((2,))],
    )(upper, *[x_parts[r] for sources in groups for r in sources], in_hbm(up), in_hbm(down))
    x_far = mirror(x_send)

    back, keeps, sends, base = {}, [], [], 0
    for sources in groups:
        size = len(sources)
        pack = held((2, row_count(size), width + hidden))
        keep, sent, *parts = call(
            functools.partial(group_kernel, size, base), (pack, pack) + (payload,) * size, 2 * flops, 2 * moved,
            in_specs=[smem()] + [vmem()] * (size + 3),
            out_specs=(vmem(),) * (size + 2),
            scratch_shapes=[pltpu.VMEM((CHUNKS, row_count(size), width), BF16)],
        )(upper, *[g_parts[r] for r in sources], pre, up_here, down_here)
        back |= dict(zip(sources, parts))
        keeps.append(keep)
        sends.append(sent)
        base += row_count(size)
    fars = [mirror(sent) for sent in sends]

    if line:
        for_far = send(back[3], [(0, 1), (3, 2)])
        across = send(back[3], [(1, 2), (2, 1)])
        both = call(add_kernel, payload, small, small, in_specs=[vmem()] * 2, out_specs=vmem())(back[2], for_far)
        skipped = swap(both, 2)
        beside = swap(back[1], 1)
        own_side, other_side = [back[0], beside], [across, skipped]
    else:
        got = [back[0]] + [swap(back[r], r) for r in range(1, owners)]
        own_side, other_side = got[:group], got[group:]

    x_chunk = pl.BlockSpec((1, rows, width), lambda k: (k, 0, 0))
    grad_up, grad_down = call(
        functools.partial(grad_kernel, len(groups)),
        (jax.ShapeDtypeStruct((model // 2, hidden), BF16), jax.ShapeDtypeStruct((hidden, model // 2), BF16)),
        2 * flops, moved,
        grid=(half,),
        in_specs=[x_chunk, x_chunk] + [vmem()] * (2 * len(groups)),
        out_specs=(pl.BlockSpec((width, hidden), lambda k: (k, 0)), pl.BlockSpec((hidden, width), lambda k: (0, k))),
    )(x_keep, x_far, *keeps, *fars)
    input_grad = call(
        functools.partial(final_kernel, len(own_side)), jax.ShapeDtypeStruct((tok, model), BF16), small, small,
        in_specs=[smem()] + [vmem()] * (owners + 1), out_specs=vmem(),
    )(mine, ids, *own_side, *other_side)
    return (input_grad[None], grad_up[None], grad_down[None])


def solution(mesh):
    placed = (
        P("pipe", "expert", None),
        P("pipe", "expert", None),
        P("pipe", "expert"),
        P("pipe", "expert", None),
        P("pipe", None, "expert"),
        P("pipe", "expert", None),
    )

    return jax.shard_map(
        per_device,
        mesh=mesh,
        in_specs=placed,
        out_specs=(P("pipe", "expert", None), P("pipe", None, "expert"), P("pipe", "expert", None)),
        check_vma=False,
    )
```

```python
import functools

import jax
import jax.numpy as jnp
from jax import lax
from jax.experimental import pallas as pl
from jax.experimental.pallas import tpu as pltpu
from jax.sharding import PartitionSpec as P


EXPERTS = 2
CAP = 34
FOLD = 8
MAIN = CAP // FOLD * FOLD
REM = CAP - MAIN
CHUNKS = FOLD // REM
LINE = 4
VMEM_LIMIT = 24 * 1024 * 1024
F32 = jnp.float32
BF16 = jnp.bfloat16


def dot(a, b, dims=((1,), (0,))):
    return lax.dot_general(a, b, (dims, ((), ())), preferred_element_type=F32)


def vmem():
    return pl.BlockSpec(memory_space=pltpu.VMEM)


def smem():
    return pl.BlockSpec(memory_space=pltpu.SMEM)


def in_hbm(value):
    return pltpu.with_memory_space_constraint(value, pltpu.HBM)


def call(kernel, outs, flops, moved, **more):
    return pl.pallas_call(
        kernel,
        out_shape=outs,
        compiler_params=pltpu.CompilerParams(vmem_limit_bytes=VMEM_LIMIT),
        cost_estimate=pl.CostEstimate(flops=flops, bytes_accessed=moved, transcendentals=0),
        **more,
    )


def route_masks(mine_ref, routes_ref):
    routes = routes_ref[...]
    tok = routes.shape[1]
    own = routes == mine_ref[0]
    own_f = jnp.where(own, 1.0, 0.0).astype(F32)
    earlier = lax.broadcasted_iota(jnp.int32, (tok, tok), 0) < lax.broadcasted_iota(jnp.int32, (tok, tok), 1)
    count_own = dot(jnp.broadcast_to(own_f, (8, tok)).astype(BF16), jnp.where(earlier, 1.0, 0.0).astype(BF16))[0:1]
    index = lax.broadcasted_iota(jnp.int32, (1, tok), 1)
    count_own = count_own.astype(jnp.int32)
    slot = jnp.where(own, count_own, index - count_own)
    rows = 2 * MAIN + 2 * FOLD
    row = lax.broadcasted_iota(jnp.int32, (rows, tok), 0)
    slot = jnp.broadcast_to(slot, (rows, tok))
    own = jnp.broadcast_to(jnp.where(own, 1, 0), (rows, tok))
    side = jnp.where(row < 2 * MAIN, row // MAIN, (row - 2 * MAIN) // FOLD)
    place = lax.rem(row, FOLD)
    hit_side = own == 1 - side
    masks = []
    for chunk in range(CHUNKS):
        folded = jnp.where(place // REM == chunk, MAIN + lax.rem(place, REM), -1)
        wanted = jnp.where(row < 2 * MAIN, lax.rem(row, MAIN), folded)
        masks.append(jnp.where(jnp.logical_and(hit_side, slot == wanted), 1.0, 0.0).astype(BF16))
    return masks


def split_rows(masks, source, own_ref, other_ref):
    width = source.shape[1] // CHUNKS
    fold_own = fold_other = None
    for chunk in range(CHUNKS):
        part = dot(masks[chunk], source[:, chunk * width:(chunk + 1) * width])
        own_ref[chunk * MAIN:(chunk + 1) * MAIN, :] = part[:MAIN].astype(BF16)
        other_ref[chunk * MAIN:(chunk + 1) * MAIN, :] = part[MAIN:2 * MAIN].astype(BF16)
        a, b = part[2 * MAIN:2 * MAIN + FOLD], part[2 * MAIN + FOLD:]
        fold_own = a if fold_own is None else fold_own + a
        fold_other = b if fold_other is None else fold_other + b
    own_ref[CHUNKS * MAIN:, :] = fold_own.astype(BF16)
    other_ref[CHUNKS * MAIN:, :] = fold_other.astype(BF16)


def hbm():
    return pl.BlockSpec(memory_space=pltpu.HBM)


def route_x_kernel(mine_ref, ids_hbm, gate_hbm, tokens_hbm, cot_hbm, own, other, masks_ref, gate, cot, ids, tokens, sems):
    copies = [
        pltpu.make_async_copy(src, dst, sems.at[i])
        for i, (src, dst) in enumerate([(ids_hbm, ids), (tokens_hbm, tokens), (gate_hbm, gate), (cot_hbm, cot)])
    ]
    for copy in copies:
        copy.start()
    copies[0].wait()
    masks = route_masks(mine_ref, ids)
    for chunk in range(CHUNKS):
        masks_ref[chunk] = masks[chunk]
    copies[1].wait()
    split_rows(masks, tokens[...], own, other)
    copies[2].wait()
    copies[3].wait()


def route_g_kernel(masks_ref, gate, cot, own, other):
    tok = gate.shape[1]
    eye = lax.broadcasted_iota(jnp.int32, (tok, tok), 0) == lax.broadcasted_iota(jnp.int32, (tok, tok), 1)
    column = jnp.sum(jnp.where(eye, jnp.broadcast_to(gate[...], (tok, tok)), 0.0), axis=1, keepdims=True)
    scaled = (column * cot[...].astype(F32)).astype(BF16)
    split_rows([masks_ref[chunk] for chunk in range(CHUNKS)], scaled, own, other)


def fold_rows(count):
    return -(-count * REM // FOLD) * FOLD


def row_count(count):
    return count * MAIN + fold_rows(count)


def fold_pick(count, chunk):
    shape = (fold_rows(count), count * FOLD)
    row = lax.broadcasted_iota(jnp.int32, shape, 0)
    col = lax.broadcasted_iota(jnp.int32, shape, 1)
    want = row // REM * FOLD + chunk * REM + lax.rem(row, REM)
    return jnp.where(col == want, 1.0, 0.0).astype(BF16)


def join_rows(payloads, rows_ref, base=0):
    count = len(payloads)
    folds = jnp.concatenate([ref[CHUNKS * MAIN:, :].astype(F32) for ref in payloads], axis=0).astype(BF16)
    last = base + count * MAIN
    for chunk in range(CHUNKS):
        for r, ref in enumerate(payloads):
            rows_ref[chunk, base + r * MAIN:base + (r + 1) * MAIN, :] = ref[chunk * MAIN:(chunk + 1) * MAIN, :]
        rows_ref[chunk, last:last + fold_rows(count), :] = dot(fold_pick(count, chunk), folds).astype(BF16)


def pick_halves(upper_ref, rows, keep_ref, send_ref):
    half = CHUNKS // 2
    upper = upper_ref[0]
    keep_ref[...] = rows[pl.ds(upper * half, half)]
    send_ref[...] = rows[pl.ds((1 - upper) * half, half)]


def times_up(rows, up_ref):
    width = rows.shape[2]
    return sum(dot(rows[chunk], up_ref[chunk * width:(chunk + 1) * width, :]) for chunk in range(CHUNKS))


def hidden_values(rows, pre, down_ref):
    width = rows.shape[2]
    dact = sum(dot(rows[chunk], down_ref[chunk * width:(chunk + 1) * width, :]) for chunk in range(CHUNKS))
    sigma = 1.0 / (1.0 + jnp.exp(-pre))
    return (dact * sigma * (1.0 + pre * (1.0 - sigma))).astype(BF16), (pre * sigma).astype(BF16)


def back_rows(dpre, up_ref, outs):
    size = len(outs)
    width = up_ref.shape[1] // CHUNKS
    folds = None
    for chunk in range(CHUNKS):
        part = dot(dpre, up_ref[:, chunk * width:(chunk + 1) * width]).astype(BF16)
        for r in range(size):
            outs[r][chunk * MAIN:(chunk + 1) * MAIN, :] = part[r * MAIN:(r + 1) * MAIN]
        fold = dot(fold_pick(size, chunk), part[size * MAIN:], ((0,), (0,)))
        folds = fold if folds is None else folds + fold
    for r in range(size):
        outs[r][CHUNKS * MAIN:, :] = folds[r * FOLD:(r + 1) * FOLD].astype(BF16)


def pre_kernel(size, upper_ref, *refs):
    payloads, (up_hbm, down_hbm, pre_ref, keep_ref, send_ref, up_ref, down_ref, rows, sems) = refs[:size], refs[size:]
    load_up = pltpu.make_async_copy(up_hbm, up_ref, sems.at[0])
    load_down = pltpu.make_async_copy(down_hbm, down_ref, sems.at[1])
    load_up.start()
    load_down.start()
    join_rows(payloads, rows)
    pick_halves(upper_ref, rows, keep_ref, send_ref)
    load_up.wait()
    pre_ref[...] = times_up(rows, up_ref)
    load_down.wait()


def flip_kernel(up_ref, down_ref, up_out, down_out):
    width = up_ref.shape[0] // CHUNKS
    for chunk in range(CHUNKS):
        at = slice(chunk * width, (chunk + 1) * width)
        up_out[:, at] = up_ref[at, :].T
        down_out[at, :] = down_ref[:, at].T


def group_kernel(size, upper_ref, *refs):
    payloads, (pre_ref, up_ref, down_ref, keep_ref, send_ref) = refs[:size], refs[size:size + 5]
    outs, rows = refs[size + 5:-1], refs[-1]
    join_rows(payloads, rows)
    width = rows.shape[2]
    pick_halves(upper_ref, rows, keep_ref.at[:, :, :width], send_ref.at[:, :, :width])
    values = hidden_values(rows, pre_ref[...], down_ref)
    for ref in (keep_ref, send_ref):
        for plane in range(2):
            ref[plane, :, width:] = values[plane]
    back_rows(values[0], up_ref, outs)


def pick_kernel(upper_ref, payload_ref, keep_ref, send_ref, rows):
    width = rows.shape[3]
    for t in range(2):
        join_rows([payload_ref.at[t]], rows.at[t])
        at = slice(t * width, (t + 1) * width)
        pick_halves(upper_ref, rows.at[t], keep_ref.at[:, :, at], send_ref.at[:, :, at])


def last_kernel(rows, up_ref, up_t_ref, down_t_ref, hidden_ref, out_ref):
    values = hidden_values(rows.at[1], times_up(rows.at[0], up_ref), down_t_ref)
    for plane in range(2):
        hidden_ref[plane] = values[plane]
    back_rows(values[0], up_t_ref, [out_ref])


def relay_kernel(inner_ref, own_x, own_g, passed_x, passed_g, out_ref):
    @pl.when(inner_ref[0] == 1)
    def _():
        out_ref[0] = passed_x[...]
        out_ref[1] = passed_g[...]

    @pl.when(inner_ref[0] == 0)
    def _():
        out_ref[0] = own_x[...]
        out_ref[1] = own_g[...]


def add_kernel(a_ref, b_ref, out_ref):
    out_ref[...] = (a_ref[...].astype(F32) + b_ref[...].astype(F32)).astype(BF16)


def grad_kernel(with_last, *refs):
    up_ref, down_ref = refs[-2:]
    xs, packs = refs[0:2], refs[2:4]
    lasts, hiddens = (refs[4:6], refs[6:8]) if with_last else ((), ())
    width = xs[0].shape[2]
    chunk = pl.program_id(0)
    across = ((0,), (0,))

    def joined(pieces):
        return jnp.concatenate(pieces, axis=0)

    x = joined([ref[0] for ref in xs] + [ref[chunk, :, :width] for ref in lasts])
    g = joined([ref[chunk, :, :width] for ref in packs] + [ref[chunk, :, width:] for ref in lasts])
    dpre, act = (joined([ref[t, :, width:] for ref in packs] + [ref[t] for ref in hiddens]) for t in range(2))
    up_ref[...] = dot(x, dpre, across).astype(BF16)
    down_ref[...] = dot(act, g, across).astype(BF16)


def final_kernel(own_count, masks_ref, *refs):
    own_refs, other_refs, out_ref = refs[:own_count], refs[own_count:-1], refs[-1]
    width = out_ref.shape[1] // CHUNKS

    def sides(lo, hi):
        return [sum(ref[lo:hi, :].astype(F32) for ref in side) for side in (own_refs, other_refs)]

    folds = sides(CHUNKS * MAIN, CHUNKS * MAIN + FOLD)
    for chunk in range(CHUNKS):
        rows = jnp.concatenate(sides(chunk * MAIN, (chunk + 1) * MAIN) + folds, axis=0).astype(BF16)
        out_ref[:, chunk * width:(chunk + 1) * width] = dot(masks_ref[chunk], rows, ((0,), (0,))).astype(BF16)


def per_device(tokens, cotangent, router_gate, routes, up_weight, down_weight):
    owners = lax.axis_size("expert")
    ranks = lax.axis_size("pipe")
    group = owners // EXPERTS
    tok, model = tokens.shape[1:]
    hidden = up_weight.shape[2]
    width = model // CHUNKS
    half = CHUNKS // 2
    here = lax.axis_index("expert")
    mine = (here // group).astype(jnp.int32).reshape(1)
    upper = (lax.axis_index("pipe") >= ranks // 2).astype(jnp.int32).reshape(1)
    ids = routes.reshape(1, tok)
    up, down = up_weight[0], down_weight[0]

    line = owners == LINE
    sources = [0, 1, 3] if line else list(range(owners))
    size = len(sources)
    rows = row_count(size)

    def held(shape, dtype=BF16):
        return pltpu.VMEM(shape, dtype)

    payload_shape = (CHUNKS * MAIN + FOLD, width)
    payload = held(payload_shape)
    halves = held((half, rows, width))

    def send(value, pairs):
        return lax.ppermute(value, "expert", pairs)

    def swap(value, r):
        return send(value, [(q, q ^ r) for q in range(owners)])

    def mirror(value):
        return lax.ppermute(value, "pipe", [(i, ranks - 1 - i) for i in range(ranks)])

    small = 1 << 20
    x_own, x_other, masks, gate, cot = call(
        route_x_kernel,
        (payload, payload, held((CHUNKS, 2 * MAIN + 2 * FOLD, tok)), held((1, tok), F32), held((tok, model))),
        small, small,
        in_specs=[smem()] + [hbm()] * 4,
        out_specs=(vmem(),) * 5,
        scratch_shapes=[pltpu.VMEM((1, tok), jnp.int32), pltpu.VMEM((tok, model), BF16), pltpu.SemaphoreType.DMA((4,))],
    )(mine, *map(in_hbm, (ids, router_gate, tokens[0], cotangent[0])))
    g_own, g_other = call(
        route_g_kernel, (payload, payload), small, small, in_specs=[vmem()] * 3, out_specs=(vmem(),) * 2
    )(masks, gate, cot)
    if line:
        x_across, x_beside = swap(x_other, 3), swap(x_own, 1)
        g_across, g_beside = swap(g_other, 3), swap(g_own, 1)
        x_parts, g_parts = [x_own, x_beside, x_across], [g_own, g_beside, g_across]
    else:
        x_parts, g_parts = (
            [own] + [swap(own if r < group else other, r) for r in range(1, owners)]
            for own, other in ((x_own, x_other), (g_own, g_other))
        )

    flops = 2 * rows * model * hidden
    moved = 2 * model * hidden
    pre, x_keep, x_send, up_here, down_here = call(
        functools.partial(pre_kernel, size),
        (held((rows, hidden), F32), halves, halves, held((model, hidden)), held((hidden, model))),
        flops, moved,
        in_specs=[smem()] + [vmem()] * size + [hbm()] * 2,
        out_specs=(vmem(),) * 5,
        scratch_shapes=[pltpu.VMEM((CHUNKS, rows, width), BF16), pltpu.SemaphoreType.DMA((2,))],
    )(upper, *x_parts, in_hbm(up), in_hbm(down))
    if line:
        inner = jnp.logical_and(here > 0, here < owners - 1).astype(jnp.int32).reshape(1)
        relayed = call(
            relay_kernel, held((2,) + payload_shape), small, small, in_specs=[smem()] + [vmem()] * 4, out_specs=vmem()
        )(inner, x_other, g_other, x_across, g_across)
        relayed = send(relayed, [(0, 2), (3, 1), (1, 0), (2, 3)])
    x_far = mirror(x_send)
    up_t, down_t = call(
        flip_kernel, (held((hidden, model)), held((model, hidden))), small, moved, in_specs=[vmem()] * 2, out_specs=(vmem(),) * 2
    )(up_here, down_here)
    pack = held((2, rows, width + hidden))
    keep, sent, *parts = call(
        functools.partial(group_kernel, size), (pack, pack) + (payload,) * size, 2 * flops, 2 * moved,
        in_specs=[smem()] + [vmem()] * (size + 3),
        out_specs=(vmem(),) * (size + 2),
        scratch_shapes=[pltpu.VMEM((CHUNKS, rows, width), BF16)],
    )(upper, *g_parts, pre, up_t, down_t)
    back = dict(zip(sources, parts))
    for_grad = [x_keep, x_far, keep, mirror(sent)]

    if line:
        one = row_count(1)
        pack = held((2, one, 2 * width))
        last_keep, last_sent, last_rows = call(
            pick_kernel, (pack, pack, held((2, CHUNKS, one, width))), small, small,
            in_specs=[smem(), vmem()],
            out_specs=(vmem(),) * 3,
        )(upper, relayed)
        last_far = mirror(last_sent)
        last_hidden, last_back = call(
            last_kernel, (held((2, one, hidden)), payload), flops, 2 * moved,
            in_specs=[vmem()] * 4,
            out_specs=(vmem(),) * 2,
        )(last_rows, up_here, up_t, down_t)
        for_grad += [last_keep, last_far, last_hidden, mirror(last_hidden)]
        for_far = send(back[3], [(0, 1), (3, 2)])
        across = send(back[3], [(1, 2), (2, 1)])
        both = call(add_kernel, payload, small, small, in_specs=[vmem()] * 2, out_specs=vmem())(last_back, for_far)
        skipped = swap(both, 2)
        own_side, other_side = [back[0], swap(back[1], 1)], [across, skipped]
    else:
        got = [back[0]] + [swap(back[r], r) for r in range(1, owners)]
        own_side, other_side = got[:group], got[group:]

    x_chunk = pl.BlockSpec((1, rows, width), lambda k: (k, 0, 0))
    grad_up, grad_down = call(
        functools.partial(grad_kernel, line),
        (jax.ShapeDtypeStruct((model // 2, hidden), BF16), jax.ShapeDtypeStruct((hidden, model // 2), BF16)),
        2 * flops, moved,
        grid=(half,),
        in_specs=[x_chunk, x_chunk] + [vmem()] * (len(for_grad) - 2),
        out_specs=(pl.BlockSpec((width, hidden), lambda k: (k, 0)), pl.BlockSpec((hidden, width), lambda k: (0, k))),
    )(*for_grad)
    input_grad = call(
        functools.partial(final_kernel, len(own_side)), jax.ShapeDtypeStruct((tok, model), BF16), small, small,
        in_specs=[vmem()] * (owners + 1), out_specs=vmem(),
    )(masks, *own_side, *other_side)
    return (input_grad[None], grad_up[None], grad_down[None])


def solution(mesh):
    placed = (
        P("pipe", "expert", None),
        P("pipe", "expert", None),
        P("pipe", "expert"),
        P("pipe", "expert", None),
        P("pipe", None, "expert"),
        P("pipe", "expert", None),
    )

    return jax.shard_map(
        per_device,
        mesh=mesh,
        in_specs=placed,
        out_specs=(P("pipe", "expert", None), P("pipe", None, "expert"), P("pipe", "expert", None)),
        check_vma=False,
    )
```

```python
import functools

import jax
import jax.numpy as jnp
from jax import lax
from jax.experimental import pallas as pl
from jax.experimental.pallas import tpu as pltpu
from jax.sharding import PartitionSpec as P


EXPERTS = 2
CAP = 34
FOLD = 8
MAIN = CAP // FOLD * FOLD
REM = CAP - MAIN
CHUNKS = FOLD // REM
LINE = 4
VMEM_LIMIT = 12 * 1024 * 1024
F32 = jnp.float32
BF16 = jnp.bfloat16


def dot(a, b, dims=((1,), (0,))):
    return lax.dot_general(a, b, (dims, ((), ())), preferred_element_type=F32)


def vmem():
    return pl.BlockSpec(memory_space=pltpu.VMEM)


def smem():
    return pl.BlockSpec(memory_space=pltpu.SMEM)


def in_hbm(value):
    return pltpu.with_memory_space_constraint(value, pltpu.HBM)


def call(kernel, outs, flops, moved, **more):
    return pl.pallas_call(
        kernel,
        out_shape=outs,
        compiler_params=pltpu.CompilerParams(vmem_limit_bytes=VMEM_LIMIT),
        cost_estimate=pl.CostEstimate(flops=flops, bytes_accessed=moved, transcendentals=0),
        **more,
    )


def route_masks(mine_ref, routes_ref):
    routes = routes_ref[...]
    tok = routes.shape[1]
    own = routes == mine_ref[0]
    own_f = jnp.where(own, 1.0, 0.0).astype(F32)
    earlier = lax.broadcasted_iota(jnp.int32, (tok, tok), 0) < lax.broadcasted_iota(jnp.int32, (tok, tok), 1)
    count_own = dot(jnp.broadcast_to(own_f, (8, tok)).astype(BF16), jnp.where(earlier, 1.0, 0.0).astype(BF16))[0:1]
    index = lax.broadcasted_iota(jnp.int32, (1, tok), 1)
    count_own = count_own.astype(jnp.int32)
    slot = jnp.where(own, count_own, index - count_own)
    rows = 2 * MAIN + 2 * FOLD
    row = lax.broadcasted_iota(jnp.int32, (rows, tok), 0)
    slot = jnp.broadcast_to(slot, (rows, tok))
    own = jnp.broadcast_to(jnp.where(own, 1, 0), (rows, tok))
    side = jnp.where(row < 2 * MAIN, row // MAIN, (row - 2 * MAIN) // FOLD)
    place = lax.rem(row, FOLD)
    hit_side = own == 1 - side
    masks = []
    for chunk in range(CHUNKS):
        folded = jnp.where(place // REM == chunk, MAIN + lax.rem(place, REM), -1)
        wanted = jnp.where(row < 2 * MAIN, lax.rem(row, MAIN), folded)
        masks.append(jnp.where(jnp.logical_and(hit_side, slot == wanted), 1.0, 0.0).astype(BF16))
    return masks


def split_rows(masks, source, own_ref, other_ref):
    width = source.shape[1] // CHUNKS
    fold_own = fold_other = None
    for chunk in range(CHUNKS):
        part = dot(masks[chunk], source[:, chunk * width:(chunk + 1) * width])
        own_ref[chunk * MAIN:(chunk + 1) * MAIN, :] = part[:MAIN].astype(BF16)
        other_ref[chunk * MAIN:(chunk + 1) * MAIN, :] = part[MAIN:2 * MAIN].astype(BF16)
        a, b = part[2 * MAIN:2 * MAIN + FOLD], part[2 * MAIN + FOLD:]
        fold_own = a if fold_own is None else fold_own + a
        fold_other = b if fold_other is None else fold_other + b
    own_ref[CHUNKS * MAIN:, :] = fold_own.astype(BF16)
    other_ref[CHUNKS * MAIN:, :] = fold_other.astype(BF16)


def hbm():
    return pl.BlockSpec(memory_space=pltpu.HBM)


def route_x_kernel(mine_ref, ids_hbm, gate_hbm, tokens_hbm, cot_hbm, own, other, masks_ref, gate, cot, ids, tokens, sems):
    copies = [
        pltpu.make_async_copy(src, dst, sems.at[i])
        for i, (src, dst) in enumerate([(ids_hbm, ids), (tokens_hbm, tokens), (gate_hbm, gate), (cot_hbm, cot)])
    ]
    for copy in copies:
        copy.start()
    copies[0].wait()
    masks = route_masks(mine_ref, ids)
    for chunk in range(CHUNKS):
        masks_ref[chunk] = masks[chunk]
    copies[1].wait()
    split_rows(masks, tokens[...], own, other)
    copies[2].wait()
    copies[3].wait()


def route_g_kernel(masks_ref, gate, cot, own, other):
    tok = gate.shape[1]
    eye = lax.broadcasted_iota(jnp.int32, (tok, tok), 0) == lax.broadcasted_iota(jnp.int32, (tok, tok), 1)
    column = jnp.sum(jnp.where(eye, jnp.broadcast_to(gate[...], (tok, tok)), 0.0), axis=1, keepdims=True)
    scaled = (column * cot[...].astype(F32)).astype(BF16)
    split_rows([masks_ref[chunk] for chunk in range(CHUNKS)], scaled, own, other)


def fold_rows(count):
    return -(-count * REM // FOLD) * FOLD


def row_count(count):
    return count * MAIN + fold_rows(count)


def fold_pick(count, chunk):
    shape = (fold_rows(count), count * FOLD)
    row = lax.broadcasted_iota(jnp.int32, shape, 0)
    col = lax.broadcasted_iota(jnp.int32, shape, 1)
    want = row // REM * FOLD + chunk * REM + lax.rem(row, REM)
    return jnp.where(col == want, 1.0, 0.0).astype(BF16)


def join_rows(payloads, rows_ref, base=0):
    count = len(payloads)
    folds = jnp.concatenate([ref[CHUNKS * MAIN:, :].astype(F32) for ref in payloads], axis=0).astype(BF16)
    last = base + count * MAIN
    for chunk in range(CHUNKS):
        for r, ref in enumerate(payloads):
            rows_ref[chunk, base + r * MAIN:base + (r + 1) * MAIN, :] = ref[chunk * MAIN:(chunk + 1) * MAIN, :]
        rows_ref[chunk, last:last + fold_rows(count), :] = dot(fold_pick(count, chunk), folds).astype(BF16)


def pick_halves(upper_ref, rows, keep_ref, send_ref):
    half = CHUNKS // 2
    upper = upper_ref[0]
    keep_ref[...] = rows[pl.ds(upper * half, half)]
    send_ref[...] = rows[pl.ds((1 - upper) * half, half)]


def chunk_of(blocks, chunk):
    return jnp.concatenate([ref[chunk] for ref in blocks], axis=0) if len(blocks) > 1 else blocks[0][chunk]


def times_up(blocks, up_ref):
    width = blocks[0].shape[2]
    return sum(dot(chunk_of(blocks, chunk), up_ref[chunk * width:(chunk + 1) * width, :]) for chunk in range(CHUNKS))


def hidden_values(blocks, pre, down_ref):
    width = blocks[0].shape[2]
    dact = sum(dot(chunk_of(blocks, chunk), down_ref[chunk * width:(chunk + 1) * width, :]) for chunk in range(CHUNKS))
    sigma = 1.0 / (1.0 + jnp.exp(-pre))
    return (dact * sigma * (1.0 + pre * (1.0 - sigma))).astype(BF16), (pre * sigma).astype(BF16)


def back_rows(dpre, up_ref, blocks):
    width = up_ref.shape[1] // CHUNKS
    folds = [None] * len(blocks)
    for chunk in range(CHUNKS):
        part = dot(dpre, up_ref[:, chunk * width:(chunk + 1) * width]).astype(BF16)
        base = 0
        for number, outs in enumerate(blocks):
            size = len(outs)
            for r in range(size):
                outs[r][chunk * MAIN:(chunk + 1) * MAIN, :] = part[base + r * MAIN:base + (r + 1) * MAIN]
            fold = dot(fold_pick(size, chunk), part[base + size * MAIN:base + row_count(size)], ((0,), (0,)))
            folds[number] = fold if folds[number] is None else folds[number] + fold
            base += row_count(size)
    for outs, fold in zip(blocks, folds):
        for r, out in enumerate(outs):
            out[CHUNKS * MAIN:, :] = fold[r * FOLD:(r + 1) * FOLD].astype(BF16)


def pre_kernel(size, upper_ref, first_ref, *refs):
    payloads, (up_hbm, down_hbm, pre_ref, keep_ref, send_ref, up_ref, down_ref, rows, sems) = refs[:size], refs[size:]
    load_up = pltpu.make_async_copy(up_hbm, up_ref, sems.at[0])
    load_down = pltpu.make_async_copy(down_hbm, down_ref, sems.at[1])
    load_up.start()
    load_down.start()
    join_rows(payloads, rows)
    pick_halves(upper_ref, rows, keep_ref, send_ref)
    load_up.wait()
    pre_ref[...] = times_up([first_ref.at[0], rows], up_ref)
    load_down.wait()


def join_kernel(size, upper_ref, *refs):
    payloads, (rows_ref, keep_ref, send_ref) = refs[:size], refs[size:]
    join_rows(payloads, rows_ref)
    pick_halves(upper_ref, rows_ref, keep_ref, send_ref)


def flip_kernel(up_ref, down_ref, up_out, down_out):
    width = up_ref.shape[0] // CHUNKS
    for chunk in range(CHUNKS):
        at = slice(chunk * width, (chunk + 1) * width)
        up_out[:, at] = up_ref[at, :].T
        down_out[at, :] = down_ref[:, at].T


def group_kernel(first_ref, rows_ref, pre_ref, up_ref, down_ref, hidden_ref, *outs):
    hidden_ref[0], hidden_ref[1] = hidden_values([first_ref.at[1], rows_ref], pre_ref[...], down_ref)
    back_rows(hidden_ref[0], up_ref, [outs[:1], outs[1:]])


def pick_kernel(upper_ref, *refs):
    payloads, (keep_ref, send_ref, rows) = refs[:-3], refs[-3:]
    if len(payloads) == 1:
        payloads = [payloads[0].at[t] for t in range(2)]
    width = rows.shape[3]
    for t in range(2):
        join_rows([payloads[t]], rows.at[t])
        at = slice(t * width, (t + 1) * width)
        pick_halves(upper_ref, rows.at[t], keep_ref.at[:, :, at], send_ref.at[:, :, at])


def last_kernel(rows, up_ref, up_t_ref, down_t_ref, hidden_ref, out_ref):
    values = hidden_values([rows.at[1]], times_up([rows.at[0]], up_ref), down_t_ref)
    for plane in range(2):
        hidden_ref[plane] = values[plane]
    back_rows(values[0], up_t_ref, [[out_ref]])


def stack_kernel(a_ref, b_ref, out_ref):
    out_ref[0] = a_ref[...]
    out_ref[1] = b_ref[...]


def add_kernel(a_ref, b_ref, out_ref):
    out_ref[...] = (a_ref[...].astype(F32) + b_ref[...].astype(F32)).astype(BF16)


ACROSS_ROWS = ((0,), (0,))


def grad_kernel(own_keep, own_far, x_keep, x_far, g_keep, g_far, hid, hid_far, up_ref, down_ref):
    width = x_keep.shape[2]
    dpre, act = (jnp.concatenate([ref[t] for ref in (hid, hid_far)], axis=0) for t in range(2))
    for chunk in range(x_keep.shape[0]):
        x, g = (
            jnp.concatenate([own_keep[chunk, :, at], keep[chunk], own_far[chunk, :, at], far[chunk]], axis=0)
            for keep, far, at in ((x_keep, x_far, slice(0, width)), (g_keep, g_far, slice(width, 2 * width)))
        )
        up_ref[chunk] = dot(x, dpre, ACROSS_ROWS).astype(up_ref.dtype)
        down_ref[chunk] = dot(act, g, ACROSS_ROWS).astype(down_ref.dtype)


def grad_last_kernel(up_part, down_part, keep, far, hid, hid_far, up_hbm, down_hbm, up_out, down_out, sems):
    width = keep.shape[2] // 2
    dpre, act = (jnp.concatenate([ref[t] for ref in (hid, hid_far)], axis=0) for t in range(2))
    copies = []
    for chunk in range(keep.shape[0]):
        x, g = (
            jnp.concatenate([ref[chunk, :, t * width:(t + 1) * width] for ref in (keep, far)], axis=0) for t in range(2)
        )
        at = slice(chunk * width, (chunk + 1) * width)
        up_out[chunk] = (up_part[chunk] + dot(x, dpre, ACROSS_ROWS)).astype(BF16)
        copies.append(pltpu.make_async_copy(up_out.at[chunk], up_hbm.at[at, :], sems.at[2 * chunk]))
        copies[-1].start()
        down_out[chunk] = (down_part[chunk] + dot(act, g, ACROSS_ROWS)).astype(BF16)
        copies.append(pltpu.make_async_copy(down_out.at[chunk], down_hbm.at[:, at], sems.at[2 * chunk + 1]))
        copies[-1].start()
    for copy in copies:
        copy.wait()


def final_kernel(own_count, masks_ref, *refs):
    own_refs, other_refs, out_ref = refs[:own_count], refs[own_count:-1], refs[-1]
    width = out_ref.shape[1] // CHUNKS

    def sides(lo, hi):
        return [sum(ref[lo:hi, :].astype(F32) for ref in side) for side in (own_refs, other_refs)]

    folds = sides(CHUNKS * MAIN, CHUNKS * MAIN + FOLD)
    for chunk in range(CHUNKS):
        rows = jnp.concatenate(sides(chunk * MAIN, (chunk + 1) * MAIN) + folds, axis=0).astype(BF16)
        out_ref[:, chunk * width:(chunk + 1) * width] = dot(masks_ref[chunk], rows, ((0,), (0,))).astype(BF16)


def per_device(tokens, cotangent, router_gate, routes, up_weight, down_weight):
    owners = lax.axis_size("expert")
    ranks = lax.axis_size("pipe")
    group = owners // EXPERTS
    tok, model = tokens.shape[1:]
    hidden = up_weight.shape[2]
    width = model // CHUNKS
    half = CHUNKS // 2
    here = lax.axis_index("expert")
    mine = (here // group).astype(jnp.int32).reshape(1)
    upper = (lax.axis_index("pipe") >= ranks // 2).astype(jnp.int32).reshape(1)
    ids = routes.reshape(1, tok)
    up, down = up_weight[0], down_weight[0]

    line = owners == LINE
    sources = [1, 2] if line else list(range(1, owners))
    size = len(sources)
    one = row_count(1)
    rows = one + row_count(size)

    def held(shape, dtype=BF16):
        return pltpu.VMEM(shape, dtype)

    payload_shape = (CHUNKS * MAIN + FOLD, width)
    payload = held(payload_shape)
    halves = held((half, row_count(size), width))
    pair = held((half, one, 2 * width))
    pair_rows = held((2, CHUNKS, one, width))

    def send(value, pairs):
        return lax.ppermute(value, "expert", pairs)

    def swap(value, r):
        return send(value, [(q, q ^ r) for q in range(owners)])

    def mirror(value):
        return lax.ppermute(value, "pipe", [(i, ranks - 1 - i) for i in range(ranks)])

    small = 1 << 20
    x_own, x_other, masks, gate, cot = call(
        route_x_kernel,
        (payload, payload, held((CHUNKS, 2 * MAIN + 2 * FOLD, tok)), held((1, tok), F32), held((tok, model))),
        small, small,
        in_specs=[smem()] + [hbm()] * 4,
        out_specs=(vmem(),) * 5,
        scratch_shapes=[pltpu.VMEM((1, tok), jnp.int32), pltpu.VMEM((tok, model), BF16), pltpu.SemaphoreType.DMA((4,))],
    )(mine, *map(in_hbm, (ids, router_gate, tokens[0], cotangent[0])))
    g_own, g_other = call(
        route_g_kernel, (payload, payload), small, small, in_specs=[vmem()] * 3, out_specs=(vmem(),) * 2
    )(masks, gate, cot)
    own_keep, own_sent, own_rows = call(
        pick_kernel, (pair, pair, pair_rows), small, small, in_specs=[smem()] + [vmem()] * 2, out_specs=(vmem(),) * 3
    )(upper, x_own, g_own)
    own_far = mirror(own_sent)
    if line:
        x_across, x_beside = swap(x_other, 2), swap(x_own, 1)
        g_across, g_beside = swap(g_other, 2), swap(g_own, 1)
        x_parts, g_parts = [x_beside, x_across], [g_beside, g_across]
    else:
        x_parts, g_parts = (
            [swap(own if r < group else other, r) for r in range(1, owners)]
            for own, other in ((x_own, x_other), (g_own, g_other))
        )

    flops = 2 * rows * model * hidden
    moved = 2 * model * hidden
    pre, x_keep, x_sent, up_here, down_here = call(
        functools.partial(pre_kernel, size),
        (held((rows, hidden), F32), halves, halves, held((model, hidden)), held((hidden, model))),
        flops, moved,
        in_specs=[smem()] + [vmem()] * (size + 1) + [hbm()] * 2,
        out_specs=(vmem(),) * 5,
        scratch_shapes=[pltpu.VMEM((CHUNKS, row_count(size), width), BF16), pltpu.SemaphoreType.DMA((2,))],
    )(upper, own_rows, *x_parts, in_hbm(up), in_hbm(down))
    if line:
        passed = call(stack_kernel, held((2,) + payload_shape), small, small, in_specs=[vmem()] * 2, out_specs=vmem())(
            x_across, g_across
        )
        passed = swap(passed, 1)
    x_far = mirror(x_sent)
    up_t, down_t = call(
        flip_kernel, (held((hidden, model)), held((model, hidden))), small, moved, in_specs=[vmem()] * 2, out_specs=(vmem(),) * 2
    )(up_here, down_here)
    g_rows, g_keep, g_sent = call(
        functools.partial(join_kernel, size), (held((CHUNKS, row_count(size), width)), halves, halves), small, small,
        in_specs=[smem()] + [vmem()] * size, out_specs=(vmem(),) * 3,
    )(upper, *g_parts)
    g_far = mirror(g_sent)
    hid, *parts = call(
        group_kernel, (held((2, rows, hidden)),) + (payload,) * (size + 1), 2 * flops, 2 * moved,
        in_specs=[vmem()] * 5, out_specs=(vmem(),) * (size + 2),
    )(own_rows, g_rows, pre, up_t, down_t)
    back = dict(zip([0] + sources, parts))
    for_grad = [own_keep, own_far, x_keep, x_far, g_keep, g_far, hid, mirror(hid)]

    if line:
        last_keep, last_sent, last_rows = call(
            pick_kernel, (pair, pair, pair_rows), small, small,
            in_specs=[smem(), vmem()],
            out_specs=(vmem(),) * 3,
        )(upper, passed)
        last_far = mirror(last_sent)
        last_hidden, last_back = call(
            last_kernel, (held((2, one, hidden)), payload), flops, 2 * moved,
            in_specs=[vmem()] * 4,
            out_specs=(vmem(),) * 2,
        )(last_rows, up_here, up_t, down_t)
        for_last = [last_keep, last_far, last_hidden, mirror(last_hidden)]
        for_far = swap(back[2], 1)
        both = call(add_kernel, payload, small, small, in_specs=[vmem()] * 2, out_specs=vmem())(last_back, for_far)
        own_side, other_side = [back[0], swap(back[1], 1)], [swap(both, 3)]
    else:
        got = [back[0]] + [swap(back[r], r) for r in range(1, owners)]
        own_side, other_side = got[:group], got[group:]

    kept = F32 if line else BF16
    grad_up, grad_down = call(
        grad_kernel, (held((half, width, hidden), kept), held((half, hidden, width), kept)), 2 * flops, moved,
        in_specs=[vmem()] * 8, out_specs=(vmem(),) * 2,
    )(*for_grad)
    if line:
        grad_up, grad_down = call(
            grad_last_kernel,
            (jax.ShapeDtypeStruct((model // 2, hidden), BF16), jax.ShapeDtypeStruct((hidden, model // 2), BF16)),
            flops, moved,
            in_specs=[vmem()] * 6, out_specs=(hbm(),) * 2,
            scratch_shapes=[
                pltpu.VMEM((half, width, hidden), BF16), pltpu.VMEM((half, hidden, width), BF16), pltpu.SemaphoreType.DMA((2 * half,))
            ],
        )(grad_up, grad_down, *for_last)
    else:
        grad_up, grad_down = grad_up.reshape(model // 2, hidden), grad_down.transpose(1, 0, 2).reshape(hidden, model // 2)
    input_grad = call(
        functools.partial(final_kernel, len(own_side)), jax.ShapeDtypeStruct((tok, model), BF16), small, small,
        in_specs=[vmem()] * (1 + len(own_side) + len(other_side)), out_specs=vmem(),
    )(masks, *own_side, *other_side)
    return (input_grad[None], grad_up[None], grad_down[None])


def solution(mesh):
    placed = (
        P("pipe", "expert", None),
        P("pipe", "expert", None),
        P("pipe", "expert"),
        P("pipe", "expert", None),
        P("pipe", None, "expert"),
        P("pipe", "expert", None),
    )

    return jax.shard_map(
        per_device,
        mesh=mesh,
        in_specs=placed,
        out_specs=(P("pipe", "expert", None), P("pipe", None, "expert"), P("pipe", "expert", None)),
        check_vma=False,
    )
```

```python
import functools

import jax
import jax.numpy as jnp
from jax import lax
from jax.experimental import pallas as pl
from jax.experimental.pallas import tpu as pltpu
from jax.sharding import PartitionSpec as P


EXPERTS = 2
CAP = 34
FOLD = 8
MAIN = CAP // FOLD * FOLD
REM = CAP - MAIN
CHUNKS = FOLD // REM
LINE = 4
VMEM_LIMIT = 12 * 1024 * 1024
F32 = jnp.float32
BF16 = jnp.bfloat16


def dot(a, b, dims=((1,), (0,))):
    return lax.dot_general(a, b, (dims, ((), ())), preferred_element_type=F32)


def vmem():
    return pl.BlockSpec(memory_space=pltpu.VMEM)


def smem():
    return pl.BlockSpec(memory_space=pltpu.SMEM)


def in_hbm(value):
    return pltpu.with_memory_space_constraint(value, pltpu.HBM)


def call(kernel, outs, flops, moved, **more):
    return pl.pallas_call(
        kernel,
        out_shape=outs,
        compiler_params=pltpu.CompilerParams(vmem_limit_bytes=VMEM_LIMIT),
        cost_estimate=pl.CostEstimate(flops=flops, bytes_accessed=moved, transcendentals=0),
        **more,
    )


def route_masks(mine_ref, routes_ref):
    routes = routes_ref[...]
    tok = routes.shape[1]
    own = routes == mine_ref[0]
    own_f = jnp.where(own, 1.0, 0.0).astype(F32)
    earlier = lax.broadcasted_iota(jnp.int32, (tok, tok), 0) < lax.broadcasted_iota(jnp.int32, (tok, tok), 1)
    count_own = dot(jnp.broadcast_to(own_f, (8, tok)).astype(BF16), jnp.where(earlier, 1.0, 0.0).astype(BF16))[0:1]
    index = lax.broadcasted_iota(jnp.int32, (1, tok), 1)
    count_own = count_own.astype(jnp.int32)
    slot = jnp.where(own, count_own, index - count_own)
    rows = 2 * MAIN + 2 * FOLD
    row = lax.broadcasted_iota(jnp.int32, (rows, tok), 0)
    slot = jnp.broadcast_to(slot, (rows, tok))
    own = jnp.broadcast_to(jnp.where(own, 1, 0), (rows, tok))
    side = jnp.where(row < 2 * MAIN, row // MAIN, (row - 2 * MAIN) // FOLD)
    place = lax.rem(row, FOLD)
    hit_side = own == 1 - side
    masks = []
    for chunk in range(CHUNKS):
        folded = jnp.where(place // REM == chunk, MAIN + lax.rem(place, REM), -1)
        wanted = jnp.where(row < 2 * MAIN, lax.rem(row, MAIN), folded)
        masks.append(jnp.where(jnp.logical_and(hit_side, slot == wanted), 1.0, 0.0).astype(BF16))
    return masks


def split_rows(masks, source, own_ref, other_ref):
    width = source.shape[1] // CHUNKS
    fold_own = fold_other = None
    for chunk in range(CHUNKS):
        part = dot(masks[chunk], source[:, chunk * width:(chunk + 1) * width])
        own_ref[chunk * MAIN:(chunk + 1) * MAIN, :] = part[:MAIN].astype(BF16)
        other_ref[chunk * MAIN:(chunk + 1) * MAIN, :] = part[MAIN:2 * MAIN].astype(BF16)
        a, b = part[2 * MAIN:2 * MAIN + FOLD], part[2 * MAIN + FOLD:]
        fold_own = a if fold_own is None else fold_own + a
        fold_other = b if fold_other is None else fold_other + b
    own_ref[CHUNKS * MAIN:, :] = fold_own.astype(BF16)
    other_ref[CHUNKS * MAIN:, :] = fold_other.astype(BF16)


def hbm():
    return pl.BlockSpec(memory_space=pltpu.HBM)


def route_x_kernel(mine_ref, ids_hbm, gate_hbm, tokens_hbm, cot_hbm, own, other, masks_ref, gate, cot, ids, tokens, sems):
    copies = [
        pltpu.make_async_copy(src, dst, sems.at[i])
        for i, (src, dst) in enumerate([(ids_hbm, ids), (tokens_hbm, tokens), (gate_hbm, gate), (cot_hbm, cot)])
    ]
    for copy in copies:
        copy.start()
    copies[0].wait()
    masks = route_masks(mine_ref, ids)
    for chunk in range(CHUNKS):
        masks_ref[chunk] = masks[chunk]
    copies[1].wait()
    split_rows(masks, tokens[...], own, other)
    copies[2].wait()
    copies[3].wait()


def route_g_kernel(masks_ref, gate, cot, own, other):
    tok = gate.shape[1]
    eye = lax.broadcasted_iota(jnp.int32, (tok, tok), 0) == lax.broadcasted_iota(jnp.int32, (tok, tok), 1)
    column = jnp.sum(jnp.where(eye, jnp.broadcast_to(gate[...], (tok, tok)), 0.0), axis=1, keepdims=True)
    scaled = (column * cot[...].astype(F32)).astype(BF16)
    split_rows([masks_ref[chunk] for chunk in range(CHUNKS)], scaled, own, other)


def fold_rows(count):
    return -(-count * REM // FOLD) * FOLD


def row_count(count):
    return count * MAIN + fold_rows(count)


def fold_pick(count, chunk):
    shape = (fold_rows(count), count * FOLD)
    row = lax.broadcasted_iota(jnp.int32, shape, 0)
    col = lax.broadcasted_iota(jnp.int32, shape, 1)
    want = row // REM * FOLD + chunk * REM + lax.rem(row, REM)
    return jnp.where(col == want, 1.0, 0.0).astype(BF16)


def join_rows(payloads, rows_ref, base=0):
    count = len(payloads)
    folds = jnp.concatenate([ref[CHUNKS * MAIN:, :].astype(F32) for ref in payloads], axis=0).astype(BF16)
    last = base + count * MAIN
    for chunk in range(CHUNKS):
        for r, ref in enumerate(payloads):
            rows_ref[chunk, base + r * MAIN:base + (r + 1) * MAIN, :] = ref[chunk * MAIN:(chunk + 1) * MAIN, :]
        rows_ref[chunk, last:last + fold_rows(count), :] = dot(fold_pick(count, chunk), folds).astype(BF16)


def pick_halves(upper_ref, rows, keep_ref, send_ref):
    half = CHUNKS // 2
    upper = upper_ref[0]
    keep_ref[...] = rows[pl.ds(upper * half, half)]
    send_ref[...] = rows[pl.ds((1 - upper) * half, half)]


def chunk_of(blocks, chunk):
    return jnp.concatenate([ref[chunk] for ref in blocks], axis=0) if len(blocks) > 1 else blocks[0][chunk]


def times_up(blocks, up_ref):
    width = blocks[0].shape[2]
    return sum(dot(chunk_of(blocks, chunk), up_ref[chunk * width:(chunk + 1) * width, :]) for chunk in range(CHUNKS))


def hidden_values(blocks, pre, down_ref):
    width = blocks[0].shape[2]
    dact = sum(dot(chunk_of(blocks, chunk), down_ref[chunk * width:(chunk + 1) * width, :]) for chunk in range(CHUNKS))
    sigma = 1.0 / (1.0 + jnp.exp(-pre))
    return (dact * sigma * (1.0 + pre * (1.0 - sigma))).astype(BF16), (pre * sigma).astype(BF16)


def back_rows(dpre, up_ref, blocks):
    width = up_ref.shape[1] // CHUNKS
    folds = [None] * len(blocks)
    for chunk in range(CHUNKS):
        part = dot(dpre, up_ref[:, chunk * width:(chunk + 1) * width]).astype(BF16)
        base = 0
        for number, outs in enumerate(blocks):
            size = len(outs)
            for r in range(size):
                outs[r][chunk * MAIN:(chunk + 1) * MAIN, :] = part[base + r * MAIN:base + (r + 1) * MAIN]
            fold = dot(fold_pick(size, chunk), part[base + size * MAIN:base + row_count(size)], ((0,), (0,)))
            folds[number] = fold if folds[number] is None else folds[number] + fold
            base += row_count(size)
    for outs, fold in zip(blocks, folds):
        for r, out in enumerate(outs):
            out[CHUNKS * MAIN:, :] = fold[r * FOLD:(r + 1) * FOLD].astype(BF16)


def pre_kernel(size, upper_ref, first_ref, *refs):
    payloads, (up_hbm, down_hbm, pre_ref, keep_ref, send_ref, up_ref, down_ref, rows, sems) = refs[:size], refs[size:]
    load_up = pltpu.make_async_copy(up_hbm, up_ref, sems.at[0])
    load_down = pltpu.make_async_copy(down_hbm, down_ref, sems.at[1])
    load_up.start()
    load_down.start()
    join_rows(payloads, rows)
    pick_halves(upper_ref, rows, keep_ref, send_ref)
    load_up.wait()
    pre_ref[...] = times_up([first_ref.at[0], rows], up_ref)
    load_down.wait()


def join_kernel(size, upper_ref, *refs):
    payloads, (rows_ref, keep_ref, send_ref) = refs[:size], refs[size:]
    join_rows(payloads, rows_ref)
    pick_halves(upper_ref, rows_ref, keep_ref, send_ref)


def flip_kernel(up_ref, down_ref, up_out, down_out):
    width = up_ref.shape[0] // CHUNKS
    for chunk in range(CHUNKS):
        at = slice(chunk * width, (chunk + 1) * width)
        up_out[:, at] = up_ref[at, :].T
        down_out[at, :] = down_ref[:, at].T


def group_kernel(first_ref, rows_ref, pre_ref, up_ref, down_ref, hidden_ref, *outs):
    hidden_ref[0], hidden_ref[1] = hidden_values([first_ref.at[1], rows_ref], pre_ref[...], down_ref)
    back_rows(hidden_ref[0], up_ref, [outs[:1], outs[1:]])


def pick_kernel(upper_ref, *refs):
    payloads, (keep_ref, send_ref, rows) = refs[:-3], refs[-3:]
    if len(payloads) == 1:
        payloads = [payloads[0].at[t] for t in range(2)]
    width = rows.shape[3]
    for t in range(2):
        join_rows([payloads[t]], rows.at[t])
        at = slice(t * width, (t + 1) * width)
        pick_halves(upper_ref, rows.at[t], keep_ref.at[:, :, at], send_ref.at[:, :, at])


def pre_last_kernel(upper_ref, payload_ref, up_ref, pre_ref, keep_ref, send_ref, rows):
    join_rows([payload_ref], rows)
    pick_halves(upper_ref, rows, keep_ref, send_ref)
    pre_ref[...] = times_up([rows], up_ref)


def last_kernel(rows, pre_ref, up_ref, down_ref, hidden_ref, out_ref):
    hidden_ref[0], hidden_ref[1] = hidden_values([rows], pre_ref[...], down_ref)
    back_rows(hidden_ref[0], up_ref, [[out_ref]])


def add_kernel(a_ref, b_ref, out_ref):
    out_ref[...] = (a_ref[...].astype(F32) + b_ref[...].astype(F32)).astype(BF16)


ACROSS_ROWS = ((0,), (0,))


def grad_kernel(own_keep, own_far, x_keep, x_far, g_keep, g_far, hid, hid_far, *refs):
    last, (up_ref, down_ref) = refs[:-2], refs[-2:]
    width = x_keep.shape[2]
    dpre, act = (jnp.concatenate([ref[t] for ref in (hid, hid_far) + last[2:]], axis=0) for t in range(2))
    for chunk in range(x_keep.shape[0]):
        x, g = (
            jnp.concatenate(
                [own_keep[chunk, :, at], keep[chunk], own_far[chunk, :, at], far[chunk]] + [ref[chunk] for ref in more], axis=0
            )
            for keep, far, at, more in (
                (x_keep, x_far, slice(0, width), last[0:1]), (g_keep, g_far, slice(width, 2 * width), last[1:2])
            )
        )
        up_ref[chunk] = dot(x, dpre, ACROSS_ROWS).astype(up_ref.dtype)
        down_ref[chunk] = dot(act, g, ACROSS_ROWS).astype(down_ref.dtype)


def grad_last_kernel(up_part, down_part, x_far, g_far, hid_far, up_hbm, down_hbm, up_out, down_out, sems):
    width = x_far.shape[2]
    dpre, act = hid_far[0], hid_far[1]
    copies = []
    for chunk in range(x_far.shape[0]):
        x, g = x_far[chunk], g_far[chunk]
        at = slice(chunk * width, (chunk + 1) * width)
        up_out[chunk] = (up_part[chunk] + dot(x, dpre, ACROSS_ROWS)).astype(BF16)
        copies.append(pltpu.make_async_copy(up_out.at[chunk], up_hbm.at[at, :], sems.at[2 * chunk]))
        copies[-1].start()
        down_out[chunk] = (down_part[chunk] + dot(act, g, ACROSS_ROWS)).astype(BF16)
        copies.append(pltpu.make_async_copy(down_out.at[chunk], down_hbm.at[:, at], sems.at[2 * chunk + 1]))
        copies[-1].start()
    for copy in copies:
        copy.wait()


def final_kernel(own_count, masks_ref, *refs):
    own_refs, other_refs, (out_hbm, out_ref, sems) = refs[:own_count], refs[own_count:-3], refs[-3:]
    width = out_ref.shape[2]
    copies = []

    def sides(lo, hi):
        return [sum(ref[lo:hi, :].astype(F32) for ref in side) for side in (own_refs, other_refs)]

    folds = sides(CHUNKS * MAIN, CHUNKS * MAIN + FOLD)
    for chunk in range(CHUNKS):
        rows = jnp.concatenate(sides(chunk * MAIN, (chunk + 1) * MAIN) + folds, axis=0).astype(BF16)
        out_ref[chunk] = dot(masks_ref[chunk], rows, ((0,), (0,))).astype(BF16)
        at = slice(chunk * width, (chunk + 1) * width)
        copies.append(pltpu.make_async_copy(out_ref.at[chunk], out_hbm.at[:, at], sems.at[chunk]))
        copies[-1].start()
    for copy in copies:
        copy.wait()


def per_device(tokens, cotangent, router_gate, routes, up_weight, down_weight):
    owners = lax.axis_size("expert")
    ranks = lax.axis_size("pipe")
    group = owners // EXPERTS
    tok, model = tokens.shape[1:]
    hidden = up_weight.shape[2]
    width = model // CHUNKS
    half = CHUNKS // 2
    here = lax.axis_index("expert")
    mine = (here // group).astype(jnp.int32).reshape(1)
    upper = (lax.axis_index("pipe") >= ranks // 2).astype(jnp.int32).reshape(1)
    ids = routes.reshape(1, tok)
    up, down = up_weight[0], down_weight[0]

    line = owners == LINE
    sources = [1, 2] if line else list(range(1, owners))
    size = len(sources)
    one = row_count(1)
    rows = one + row_count(size)

    def held(shape, dtype=BF16):
        return pltpu.VMEM(shape, dtype)

    payload_shape = (CHUNKS * MAIN + FOLD, width)
    payload = held(payload_shape)
    halves = held((half, row_count(size), width))
    pair = held((half, one, 2 * width))
    pair_rows = held((2, CHUNKS, one, width))

    def send(value, pairs):
        return lax.ppermute(value, "expert", pairs)

    def swap(value, r):
        return send(value, [(q, q ^ r) for q in range(owners)])

    def mirror(value):
        return lax.ppermute(value, "pipe", [(i, ranks - 1 - i) for i in range(ranks)])

    small = 1 << 20
    x_own, x_other, masks, gate, cot = call(
        route_x_kernel,
        (payload, payload, held((CHUNKS, 2 * MAIN + 2 * FOLD, tok)), held((1, tok), F32), held((tok, model))),
        small, small,
        in_specs=[smem()] + [hbm()] * 4,
        out_specs=(vmem(),) * 5,
        scratch_shapes=[pltpu.VMEM((1, tok), jnp.int32), pltpu.VMEM((tok, model), BF16), pltpu.SemaphoreType.DMA((4,))],
    )(mine, *map(in_hbm, (ids, router_gate, tokens[0], cotangent[0])))
    g_own, g_other = call(
        route_g_kernel, (payload, payload), small, small, in_specs=[vmem()] * 3, out_specs=(vmem(),) * 2
    )(masks, gate, cot)
    own_keep, own_sent, own_rows = call(
        pick_kernel, (pair, pair, pair_rows), small, small, in_specs=[smem()] + [vmem()] * 2, out_specs=(vmem(),) * 3
    )(upper, x_own, g_own)
    own_far = mirror(own_sent)
    if line:
        x_across, x_beside = swap(x_other, 2), swap(x_own, 1)
        g_across, g_beside = swap(g_other, 2), swap(g_own, 1)
        x_parts, g_parts = [x_beside, x_across], [g_beside, g_across]
    else:
        x_parts, g_parts = (
            [swap(own if r < group else other, r) for r in range(1, owners)]
            for own, other in ((x_own, x_other), (g_own, g_other))
        )

    flops = 2 * rows * model * hidden
    moved = 2 * model * hidden
    pre, x_keep, x_sent, up_here, down_here = call(
        functools.partial(pre_kernel, size),
        (held((rows, hidden), F32), halves, halves, held((model, hidden)), held((hidden, model))),
        flops, moved,
        in_specs=[smem()] + [vmem()] * (size + 1) + [hbm()] * 2,
        out_specs=(vmem(),) * 5,
        scratch_shapes=[pltpu.VMEM((CHUNKS, row_count(size), width), BF16), pltpu.SemaphoreType.DMA((2,))],
    )(upper, own_rows, *x_parts, in_hbm(up), in_hbm(down))
    if line:
        x_passed, g_passed = swap(x_across, 1), swap(g_across, 1)
    x_far = mirror(x_sent)
    up_t, down_t = call(
        flip_kernel, (held((hidden, model)), held((model, hidden))), small, moved, in_specs=[vmem()] * 2, out_specs=(vmem(),) * 2
    )(up_here, down_here)
    g_rows, g_keep, g_sent = call(
        functools.partial(join_kernel, size), (held((CHUNKS, row_count(size), width)), halves, halves), small, small,
        in_specs=[smem()] + [vmem()] * size, out_specs=(vmem(),) * 3,
    )(upper, *g_parts)
    g_far = mirror(g_sent)
    hid, *parts = call(
        group_kernel, (held((2, rows, hidden)),) + (payload,) * (size + 1), 2 * flops, 2 * moved,
        in_specs=[vmem()] * 5, out_specs=(vmem(),) * (size + 2),
    )(own_rows, g_rows, pre, up_t, down_t)
    back = dict(zip([0] + sources, parts))
    for_grad = [own_keep, own_far, x_keep, x_far, g_keep, g_far, hid, mirror(hid)]

    if line:
        single = held((half, one, width))
        last_pre, xl_keep, xl_sent = call(
            pre_last_kernel, (held((one, hidden), F32), single, single), flops, moved,
            in_specs=[smem()] + [vmem()] * 2, out_specs=(vmem(),) * 3,
            scratch_shapes=[pltpu.VMEM((CHUNKS, one, width), BF16)],
        )(upper, x_passed, up_here)
        xl_far = mirror(xl_sent)
        last_rows, gl_keep, gl_sent = call(
            functools.partial(join_kernel, 1), (held((CHUNKS, one, width)), single, single), small, small,
            in_specs=[smem(), vmem()], out_specs=(vmem(),) * 3,
        )(upper, g_passed)
        gl_far = mirror(gl_sent)
        last_hidden, last_back = call(
            last_kernel, (held((2, one, hidden)), payload), flops, 2 * moved,
            in_specs=[vmem()] * 4,
            out_specs=(vmem(),) * 2,
        )(last_rows, last_pre, up_t, down_t)
        for_grad += [xl_keep, gl_keep, last_hidden]
        for_last = [xl_far, gl_far, mirror(last_hidden)]
        for_far = swap(back[2], 1)
        both = call(add_kernel, payload, small, small, in_specs=[vmem()] * 2, out_specs=vmem())(last_back, for_far)
        own_side, other_side = [back[0], swap(back[1], 1)], [swap(both, 3)]
    else:
        got = [back[0]] + [swap(back[r], r) for r in range(1, owners)]
        own_side, other_side = got[:group], got[group:]

    kept = F32 if line else BF16
    grad_up, grad_down = call(
        grad_kernel, (held((half, width, hidden), kept), held((half, hidden, width), kept)), 2 * flops, moved,
        in_specs=[vmem()] * len(for_grad), out_specs=(vmem(),) * 2,
    )(*for_grad)
    if line:
        grad_up, grad_down = call(
            grad_last_kernel,
            (jax.ShapeDtypeStruct((model // 2, hidden), BF16), jax.ShapeDtypeStruct((hidden, model // 2), BF16)),
            flops, moved,
            in_specs=[vmem()] * 5, out_specs=(hbm(),) * 2,
            scratch_shapes=[
                pltpu.VMEM((half, width, hidden), BF16), pltpu.VMEM((half, hidden, width), BF16), pltpu.SemaphoreType.DMA((2 * half,))
            ],
        )(grad_up, grad_down, *for_last)
    else:
        grad_up, grad_down = grad_up.reshape(model // 2, hidden), grad_down.transpose(1, 0, 2).reshape(hidden, model // 2)
    input_grad = call(
        functools.partial(final_kernel, len(own_side)), jax.ShapeDtypeStruct((tok, model), BF16), small, small,
        in_specs=[vmem()] * (1 + len(own_side) + len(other_side)), out_specs=hbm(),
        scratch_shapes=[pltpu.VMEM((CHUNKS, tok, width), BF16), pltpu.SemaphoreType.DMA((CHUNKS,))],
    )(masks, *own_side, *other_side)
    return (input_grad[None], grad_up[None], grad_down[None])


def solution(mesh):
    placed = (
        P("pipe", "expert", None),
        P("pipe", "expert", None),
        P("pipe", "expert"),
        P("pipe", "expert", None),
        P("pipe", None, "expert"),
        P("pipe", "expert", None),
    )

    return jax.shard_map(
        per_device,
        mesh=mesh,
        in_specs=placed,
        out_specs=(P("pipe", "expert", None), P("pipe", None, "expert"), P("pipe", "expert", None)),
        check_vma=False,
    )
```

```python
import functools

import jax
import jax.numpy as jnp
from jax import lax
from jax.experimental import pallas as pl
from jax.experimental.pallas import tpu as pltpu
from jax.sharding import PartitionSpec as P


EXPERTS = 2
CAP = 34
FOLD = 8
MAIN = CAP // FOLD * FOLD
REM = CAP - MAIN
CHUNKS = FOLD // REM
LINE = 4
VMEM_LIMIT = 12 * 1024 * 1024
F32 = jnp.float32
BF16 = jnp.bfloat16


def dot(a, b, dims=((1,), (0,))):
    return lax.dot_general(a, b, (dims, ((), ())), preferred_element_type=F32)


def vmem():
    return pl.BlockSpec(memory_space=pltpu.VMEM)


def smem():
    return pl.BlockSpec(memory_space=pltpu.SMEM)


def in_hbm(value):
    return pltpu.with_memory_space_constraint(value, pltpu.HBM)


def call(kernel, outs, flops, moved, **more):
    return pl.pallas_call(
        kernel,
        out_shape=outs,
        compiler_params=pltpu.CompilerParams(vmem_limit_bytes=VMEM_LIMIT),
        cost_estimate=pl.CostEstimate(flops=flops, bytes_accessed=moved, transcendentals=0),
        **more,
    )


def route_masks(mine_ref, routes_ref):
    routes = routes_ref[...]
    tok = routes.shape[1]
    own = routes == mine_ref[0]
    own_f = jnp.where(own, 1.0, 0.0).astype(F32)
    earlier = lax.broadcasted_iota(jnp.int32, (tok, tok), 0) < lax.broadcasted_iota(jnp.int32, (tok, tok), 1)
    count_own = dot(jnp.broadcast_to(own_f, (8, tok)).astype(BF16), jnp.where(earlier, 1.0, 0.0).astype(BF16))[0:1]
    index = lax.broadcasted_iota(jnp.int32, (1, tok), 1)
    count_own = count_own.astype(jnp.int32)
    slot = jnp.where(own, count_own, index - count_own)
    rows = 2 * MAIN + 2 * FOLD
    row = lax.broadcasted_iota(jnp.int32, (rows, tok), 0)
    slot = jnp.broadcast_to(slot, (rows, tok))
    own = jnp.broadcast_to(jnp.where(own, 1, 0), (rows, tok))
    side = jnp.where(row < 2 * MAIN, row // MAIN, (row - 2 * MAIN) // FOLD)
    place = lax.rem(row, FOLD)
    hit_side = own == 1 - side
    masks = []
    for chunk in range(CHUNKS):
        folded = jnp.where(place // REM == chunk, MAIN + lax.rem(place, REM), -1)
        wanted = jnp.where(row < 2 * MAIN, lax.rem(row, MAIN), folded)
        masks.append(jnp.where(jnp.logical_and(hit_side, slot == wanted), 1.0, 0.0).astype(BF16))
    return masks


def split_rows(masks, source, own_ref, other_ref):
    width = source.shape[1] // CHUNKS
    fold_own = fold_other = None
    for chunk in range(CHUNKS):
        part = dot(masks[chunk], source[:, chunk * width:(chunk + 1) * width])
        own_ref[chunk * MAIN:(chunk + 1) * MAIN, :] = part[:MAIN].astype(BF16)
        other_ref[chunk * MAIN:(chunk + 1) * MAIN, :] = part[MAIN:2 * MAIN].astype(BF16)
        a, b = part[2 * MAIN:2 * MAIN + FOLD], part[2 * MAIN + FOLD:]
        fold_own = a if fold_own is None else fold_own + a
        fold_other = b if fold_other is None else fold_other + b
    own_ref[CHUNKS * MAIN:, :] = fold_own.astype(BF16)
    other_ref[CHUNKS * MAIN:, :] = fold_other.astype(BF16)


def hbm():
    return pl.BlockSpec(memory_space=pltpu.HBM)


def route_x_kernel(mine_ref, ids_hbm, gate_hbm, tokens_hbm, cot_hbm, own, other, masks_ref, gate, cot, ids, tokens, sems):
    copies = [
        pltpu.make_async_copy(src, dst, sems.at[i])
        for i, (src, dst) in enumerate([(ids_hbm, ids), (tokens_hbm, tokens), (gate_hbm, gate), (cot_hbm, cot)])
    ]
    for copy in copies:
        copy.start()
    copies[0].wait()
    masks = route_masks(mine_ref, ids)
    for chunk in range(CHUNKS):
        masks_ref[chunk] = masks[chunk]
    copies[1].wait()
    split_rows(masks, tokens[...], own, other)
    copies[2].wait()
    copies[3].wait()


def route_g_kernel(masks_ref, gate, cot, own, other):
    tok = gate.shape[1]
    eye = lax.broadcasted_iota(jnp.int32, (tok, tok), 0) == lax.broadcasted_iota(jnp.int32, (tok, tok), 1)
    column = jnp.sum(jnp.where(eye, jnp.broadcast_to(gate[...], (tok, tok)), 0.0), axis=1, keepdims=True)
    scaled = (column * cot[...].astype(F32)).astype(BF16)
    split_rows([masks_ref[chunk] for chunk in range(CHUNKS)], scaled, own, other)


def fold_rows(count):
    return -(-count * REM // FOLD) * FOLD


def row_count(count):
    return count * MAIN + fold_rows(count)


def fold_pick(count, chunk):
    shape = (fold_rows(count), count * FOLD)
    row = lax.broadcasted_iota(jnp.int32, shape, 0)
    col = lax.broadcasted_iota(jnp.int32, shape, 1)
    want = row // REM * FOLD + chunk * REM + lax.rem(row, REM)
    return jnp.where(col == want, 1.0, 0.0).astype(BF16)


def join_rows(payloads, rows_ref, base=0):
    count = len(payloads)
    folds = jnp.concatenate([ref[CHUNKS * MAIN:, :].astype(F32) for ref in payloads], axis=0).astype(BF16)
    last = base + count * MAIN
    for chunk in range(CHUNKS):
        for r, ref in enumerate(payloads):
            rows_ref[chunk, base + r * MAIN:base + (r + 1) * MAIN, :] = ref[chunk * MAIN:(chunk + 1) * MAIN, :]
        rows_ref[chunk, last:last + fold_rows(count), :] = dot(fold_pick(count, chunk), folds).astype(BF16)


def pick_halves(upper_ref, rows, keep_ref, send_ref):
    half = CHUNKS // 2
    upper = upper_ref[0]
    keep_ref[...] = rows[pl.ds(upper * half, half)]
    send_ref[...] = rows[pl.ds((1 - upper) * half, half)]


def chunk_of(blocks, chunk):
    return jnp.concatenate([ref[chunk] for ref in blocks], axis=0) if len(blocks) > 1 else blocks[0][chunk]


def times_up(blocks, up_ref):
    width = blocks[0].shape[2]
    return sum(dot(chunk_of(blocks, chunk), up_ref[chunk * width:(chunk + 1) * width, :]) for chunk in range(CHUNKS))


def hidden_values(blocks, pre, down_ref):
    width = blocks[0].shape[2]
    dact = sum(dot(chunk_of(blocks, chunk), down_ref[chunk * width:(chunk + 1) * width, :]) for chunk in range(CHUNKS))
    sigma = 1.0 / (1.0 + jnp.exp(-pre))
    return (dact * sigma * (1.0 + pre * (1.0 - sigma))).astype(BF16), (pre * sigma).astype(BF16)


def back_rows(dpre, up_ref, blocks):
    width = up_ref.shape[1] // CHUNKS
    folds = [None] * len(blocks)
    for chunk in range(CHUNKS):
        part = dot(dpre, up_ref[:, chunk * width:(chunk + 1) * width]).astype(BF16)
        base = 0
        for number, outs in enumerate(blocks):
            size = len(outs)
            for r in range(size):
                outs[r][chunk * MAIN:(chunk + 1) * MAIN, :] = part[base + r * MAIN:base + (r + 1) * MAIN]
            fold = dot(fold_pick(size, chunk), part[base + size * MAIN:base + row_count(size)], ((0,), (0,)))
            folds[number] = fold if folds[number] is None else folds[number] + fold
            base += row_count(size)
    for outs, fold in zip(blocks, folds):
        for r, out in enumerate(outs):
            out[CHUNKS * MAIN:, :] = fold[r * FOLD:(r + 1) * FOLD].astype(BF16)


def pre_kernel(size, upper_ref, first_ref, *refs):
    payloads, (up_hbm, down_hbm, pre_ref, keep_ref, send_ref, up_ref, down_ref, rows, sems) = refs[:size], refs[size:]
    load_up = pltpu.make_async_copy(up_hbm, up_ref, sems.at[0])
    load_down = pltpu.make_async_copy(down_hbm, down_ref, sems.at[1])
    load_up.start()
    load_down.start()
    join_rows(payloads, rows)
    pick_halves(upper_ref, rows, keep_ref, send_ref)
    load_up.wait()
    pre_ref[...] = times_up([first_ref.at[0], rows], up_ref)
    load_down.wait()


def join_kernel(size, upper_ref, *refs):
    payloads, (rows_ref, keep_ref, send_ref) = refs[:size], refs[size:]
    join_rows(payloads, rows_ref)
    pick_halves(upper_ref, rows_ref, keep_ref, send_ref)


def flip_kernel(up_ref, down_ref, up_out, down_out):
    width = up_ref.shape[0] // CHUNKS
    for chunk in range(CHUNKS):
        at = slice(chunk * width, (chunk + 1) * width)
        up_out[:, at] = up_ref[at, :].T
        down_out[at, :] = down_ref[:, at].T


def group_kernel(first_ref, rows_ref, pre_ref, up_ref, down_ref, hidden_ref, *outs):
    hidden_ref[0], hidden_ref[1] = hidden_values([first_ref.at[1], rows_ref], pre_ref[...], down_ref)
    back_rows(hidden_ref[0], up_ref, [outs[:1], outs[1:]])


def pick_kernel(upper_ref, *refs):
    payloads, (keep_ref, send_ref, rows) = refs[:-3], refs[-3:]
    if len(payloads) == 1:
        payloads = [payloads[0].at[t] for t in range(2)]
    width = rows.shape[3]
    for t in range(2):
        join_rows([payloads[t]], rows.at[t])
        at = slice(t * width, (t + 1) * width)
        pick_halves(upper_ref, rows.at[t], keep_ref.at[:, :, at], send_ref.at[:, :, at])


def pre_last_kernel(upper_ref, payload_ref, up_ref, pre_ref, keep_ref, send_ref, rows):
    join_rows([payload_ref], rows)
    pick_halves(upper_ref, rows, keep_ref, send_ref)
    pre_ref[...] = times_up([rows], up_ref)


def last_kernel(rows, pre_ref, up_ref, down_ref, hidden_ref, out_ref):
    hidden_ref[0], hidden_ref[1] = hidden_values([rows], pre_ref[...], down_ref)
    back_rows(hidden_ref[0], up_ref, [[out_ref]])


def add_kernel(a_ref, b_ref, out_ref):
    out_ref[...] = (a_ref[...].astype(F32) + b_ref[...].astype(F32)).astype(BF16)


ACROSS_ROWS = ((0,), (0,))


def grad_kernel(own_keep, own_far, x_keep, x_far, g_keep, g_far, hid, hid_far, up_ref, down_ref):
    width = x_keep.shape[2]
    dpre, act = (jnp.concatenate([ref[t] for ref in (hid, hid_far)], axis=0) for t in range(2))
    for chunk in range(x_keep.shape[0]):
        x, g = (
            jnp.concatenate([own_keep[chunk, :, at], keep[chunk], own_far[chunk, :, at], far[chunk]], axis=0)
            for keep, far, at in ((x_keep, x_far, slice(0, width)), (g_keep, g_far, slice(width, 2 * width)))
        )
        up_ref[chunk] = dot(x, dpre, ACROSS_ROWS).astype(up_ref.dtype)
        down_ref[chunk] = dot(act, g, ACROSS_ROWS).astype(down_ref.dtype)


def grad_last_kernel(up_part, down_part, x_keep, x_far, g_keep, g_far, hid, hid_far, up_hbm, down_hbm, up_out, down_out, sems):
    width = x_keep.shape[2]
    dpre, act = (jnp.concatenate([ref[t] for ref in (hid, hid_far)], axis=0) for t in range(2))
    copies = []
    for chunk in range(x_keep.shape[0]):
        x, g = (jnp.concatenate([ref[chunk] for ref in refs], axis=0) for refs in ((x_keep, x_far), (g_keep, g_far)))
        at = slice(chunk * width, (chunk + 1) * width)
        up_out[chunk] = (up_part[chunk] + dot(x, dpre, ACROSS_ROWS)).astype(BF16)
        copies.append(pltpu.make_async_copy(up_out.at[chunk], up_hbm.at[at, :], sems.at[2 * chunk]))
        copies[-1].start()
        down_out[chunk] = (down_part[chunk] + dot(act, g, ACROSS_ROWS)).astype(BF16)
        copies.append(pltpu.make_async_copy(down_out.at[chunk], down_hbm.at[:, at], sems.at[2 * chunk + 1]))
        copies[-1].start()
    for copy in copies:
        copy.wait()


def final_kernel(own_count, masks_ref, *refs):
    own_refs, other_refs, out_ref = refs[:own_count], refs[own_count:-1], refs[-1]
    width = out_ref.shape[1] // CHUNKS

    def sides(lo, hi):
        return [sum(ref[lo:hi, :].astype(F32) for ref in side) for side in (own_refs, other_refs)]

    folds = sides(CHUNKS * MAIN, CHUNKS * MAIN + FOLD)
    for chunk in range(CHUNKS):
        rows = jnp.concatenate(sides(chunk * MAIN, (chunk + 1) * MAIN) + folds, axis=0).astype(BF16)
        out_ref[:, chunk * width:(chunk + 1) * width] = dot(masks_ref[chunk], rows, ((0,), (0,))).astype(BF16)


def per_device(tokens, cotangent, router_gate, routes, up_weight, down_weight):
    owners = lax.axis_size("expert")
    ranks = lax.axis_size("pipe")
    group = owners // EXPERTS
    tok, model = tokens.shape[1:]
    hidden = up_weight.shape[2]
    width = model // CHUNKS
    half = CHUNKS // 2
    here = lax.axis_index("expert")
    mine = (here // group).astype(jnp.int32).reshape(1)
    upper = (lax.axis_index("pipe") >= ranks // 2).astype(jnp.int32).reshape(1)
    ids = routes.reshape(1, tok)
    up, down = up_weight[0], down_weight[0]

    line = owners == LINE
    sources = [1, 2] if line else list(range(1, owners))
    size = len(sources)
    one = row_count(1)
    rows = one + row_count(size)

    def held(shape, dtype=BF16):
        return pltpu.VMEM(shape, dtype)

    payload_shape = (CHUNKS * MAIN + FOLD, width)
    payload = held(payload_shape)
    halves = held((half, row_count(size), width))
    pair = held((half, one, 2 * width))
    pair_rows = held((2, CHUNKS, one, width))

    def send(value, pairs):
        return lax.ppermute(value, "expert", pairs)

    def swap(value, r):
        return send(value, [(q, q ^ r) for q in range(owners)])

    def mirror(value):
        return lax.ppermute(value, "pipe", [(i, ranks - 1 - i) for i in range(ranks)])

    small = 1 << 20
    x_own, x_other, masks, gate, cot = call(
        route_x_kernel,
        (payload, payload, held((CHUNKS, 2 * MAIN + 2 * FOLD, tok)), held((1, tok), F32), held((tok, model))),
        small, small,
        in_specs=[smem()] + [hbm()] * 4,
        out_specs=(vmem(),) * 5,
        scratch_shapes=[pltpu.VMEM((1, tok), jnp.int32), pltpu.VMEM((tok, model), BF16), pltpu.SemaphoreType.DMA((4,))],
    )(mine, *map(in_hbm, (ids, router_gate, tokens[0], cotangent[0])))
    g_own, g_other = call(
        route_g_kernel, (payload, payload), small, small, in_specs=[vmem()] * 3, out_specs=(vmem(),) * 2
    )(masks, gate, cot)
    own_keep, own_sent, own_rows = call(
        pick_kernel, (pair, pair, pair_rows), small, small, in_specs=[smem()] + [vmem()] * 2, out_specs=(vmem(),) * 3
    )(upper, x_own, g_own)
    own_far = mirror(own_sent)
    if line:
        x_across, x_beside = swap(x_other, 2), swap(x_own, 1)
        g_across, g_beside = swap(g_other, 2), swap(g_own, 1)
        x_parts, g_parts = [x_beside, x_across], [g_beside, g_across]
    else:
        x_parts, g_parts = (
            [swap(own if r < group else other, r) for r in range(1, owners)]
            for own, other in ((x_own, x_other), (g_own, g_other))
        )

    flops = 2 * rows * model * hidden
    moved = 2 * model * hidden
    pre, x_keep, x_sent, up_here, down_here = call(
        functools.partial(pre_kernel, size),
        (held((rows, hidden), F32), halves, halves, held((model, hidden)), held((hidden, model))),
        flops, moved,
        in_specs=[smem()] + [vmem()] * (size + 1) + [hbm()] * 2,
        out_specs=(vmem(),) * 5,
        scratch_shapes=[pltpu.VMEM((CHUNKS, row_count(size), width), BF16), pltpu.SemaphoreType.DMA((2,))],
    )(upper, own_rows, *x_parts, in_hbm(up), in_hbm(down))
    if line:
        x_passed, g_passed = swap(x_across, 1), swap(g_across, 1)
    x_far = mirror(x_sent)
    up_t, down_t = call(
        flip_kernel, (held((hidden, model)), held((model, hidden))), small, moved, in_specs=[vmem()] * 2, out_specs=(vmem(),) * 2
    )(up_here, down_here)
    g_rows, g_keep, g_sent = call(
        functools.partial(join_kernel, size), (held((CHUNKS, row_count(size), width)), halves, halves), small, small,
        in_specs=[smem()] + [vmem()] * size, out_specs=(vmem(),) * 3,
    )(upper, *g_parts)
    g_far = mirror(g_sent)
    hid, *parts = call(
        group_kernel, (held((2, rows, hidden)),) + (payload,) * (size + 1), 2 * flops, 2 * moved,
        in_specs=[vmem()] * 5, out_specs=(vmem(),) * (size + 2),
    )(own_rows, g_rows, pre, up_t, down_t)
    back = dict(zip([0] + sources, parts))
    for_grad = [own_keep, own_far, x_keep, x_far, g_keep, g_far, hid, mirror(hid)]

    if line:
        single = held((half, one, width))
        last_pre, xl_keep, xl_sent = call(
            pre_last_kernel, (held((one, hidden), F32), single, single), flops, moved,
            in_specs=[smem()] + [vmem()] * 2, out_specs=(vmem(),) * 3,
            scratch_shapes=[pltpu.VMEM((CHUNKS, one, width), BF16)],
        )(upper, x_passed, up_here)
        xl_far = mirror(xl_sent)
        last_rows, gl_keep, gl_sent = call(
            functools.partial(join_kernel, 1), (held((CHUNKS, one, width)), single, single), small, small,
            in_specs=[smem(), vmem()], out_specs=(vmem(),) * 3,
        )(upper, g_passed)
        gl_far = mirror(gl_sent)
        last_hidden, last_back = call(
            last_kernel, (held((2, one, hidden)), payload), flops, 2 * moved,
            in_specs=[vmem()] * 4,
            out_specs=(vmem(),) * 2,
        )(last_rows, last_pre, up_t, down_t)
        for_last = [xl_keep, xl_far, gl_keep, gl_far, last_hidden, mirror(last_hidden)]
        for_far = swap(back[2], 1)
        both = call(add_kernel, payload, small, small, in_specs=[vmem()] * 2, out_specs=vmem())(last_back, for_far)
        own_side, other_side = [back[0], swap(back[1], 1)], [swap(both, 3)]
    else:
        got = [back[0]] + [swap(back[r], r) for r in range(1, owners)]
        own_side, other_side = got[:group], got[group:]

    kept = F32 if line else BF16
    grad_up, grad_down = call(
        grad_kernel, (held((half, width, hidden), kept), held((half, hidden, width), kept)), 2 * flops, moved,
        in_specs=[vmem()] * 8, out_specs=(vmem(),) * 2,
    )(*for_grad)
    if line:
        grad_up, grad_down = call(
            grad_last_kernel,
            (jax.ShapeDtypeStruct((model // 2, hidden), BF16), jax.ShapeDtypeStruct((hidden, model // 2), BF16)),
            flops, moved,
            in_specs=[vmem()] * 8, out_specs=(hbm(),) * 2,
            scratch_shapes=[
                pltpu.VMEM((half, width, hidden), BF16), pltpu.VMEM((half, hidden, width), BF16), pltpu.SemaphoreType.DMA((2 * half,))
            ],
        )(grad_up, grad_down, *for_last)
    else:
        grad_up, grad_down = grad_up.reshape(model // 2, hidden), grad_down.transpose(1, 0, 2).reshape(hidden, model // 2)
    input_grad = call(
        functools.partial(final_kernel, len(own_side)), jax.ShapeDtypeStruct((tok, model), BF16), small, small,
        in_specs=[vmem()] * (1 + len(own_side) + len(other_side)), out_specs=vmem(),
    )(masks, *own_side, *other_side)
    return (input_grad[None], grad_up[None], grad_down[None])


def solution(mesh):
    placed = (
        P("pipe", "expert", None),
        P("pipe", "expert", None),
        P("pipe", "expert"),
        P("pipe", "expert", None),
        P("pipe", None, "expert"),
        P("pipe", "expert", None),
    )

    return jax.shard_map(
        per_device,
        mesh=mesh,
        in_specs=placed,
        out_specs=(P("pipe", "expert", None), P("pipe", None, "expert"), P("pipe", "expert", None)),
        check_vma=False,
    )
```
